512 devices in a mesh: dp: 16 (over x, y), mp: 32 (over z, core).
Axes of the slice: x: 4, y: 4, z: 16, core: 2. Of those that a mesh axis runs over, the one named last changes fastest.
Arguments:
- hidden_policy: bfloat16 [256, 16, 2048], P('dp', None, 'mp'), may hold values from -6 to 6
- hidden_reference: bfloat16 [256, 16, 2048], P('dp', None, 'mp'), may hold values from -6 to 6
- ffn_gain_policy: float32 [2048], replicated, may hold values from 0.1 to 1.9
- ffn_gain_reference: float32 [2048], replicated, may hold values from 0.1 to 1.9
- up_policy: bfloat16 [2048, 4096], P(None, 'mp'), may hold values from -0.125 to 0.125
- up_reference: bfloat16 [2048, 4096], P(None, 'mp'), may hold values from -0.125 to 0.125
- down_policy: bfloat16 [4096, 2048], P('mp'), may hold values from -0.1875 to 0.1875
- down_reference: bfloat16 [4096, 2048], P('mp'), may hold values from -0.1875 to 0.1875
- final_gain_policy: float32 [2048], replicated, may hold values from 0.1 to 1.9
- final_gain_reference: float32 [2048], replicated, may hold values from 0.1 to 1.9
- out_policy: bfloat16 [2048, 28672], P('dp', 'mp'), may hold values from -4 to 4
- out_reference: bfloat16 [2048, 28672], P('dp', 'mp'), may hold values from -4 to 4
- move_plan: int32 [256], replicated, may hold values from 0 to 255, as said below
- lengths: int32 [256], P('dp'), may hold values from 1 to 16, 2048 in all
- targets: int32 [256, 16], P('dp'), may hold values from 0 to 28671
Outputs:
- token_diff: float32 [256, 16], P('dp')
- seq_diff: float32 [256], P('dp')
The draws below stay inside these ranges and needn't reach their ends.
Inputs may be any that keep to these rules, and one draw needn't show every extreme that they name: `move_plan`: A permutation of the slots; slot // 16 is the owning index of dp, each owning exactly 16 requests; from one index of dp to one owner go either no requests or exactly 2.
All inputs are finite; a program needn't handle non-finite values. No bound on the sum of `lengths` on one device may be relied on, other than what follows from the above.
Results may differ from the reference program's by a relative error of at most 0.0081.
Values may be sent and summed in bfloat16 or wider, within the bound.
A program may use at most 64 MiB of HBM per device.

```python
import math
import jax
import jax.numpy as jnp
import numpy as np
from jax import lax

D = 2048
FF = 4096
REQ_DEV = 16
SEQ = 16
VOCAB = 28672
REQS = 256
CAP = 2


def shared_patterns(key):
    base = jax.random.fold_in(key, 909)
    first, second = jax.random.split(base, 2)
    signs = jnp.where(jax.random.bernoulli(first, 0.5, (3, D)), 1.0, -1.0).astype(jnp.float32)
    stride = VOCAB // 6
    shifts = jax.random.randint(second, (6,), 0, stride).astype(jnp.int32)
    columns = jnp.arange(6, dtype=jnp.int32) * stride + shifts
    return (signs, columns)


def hidden_matrix(key, salt):
    base = jax.random.fold_in(key, salt)
    values = jax.random.normal(base, (REQS, SEQ, D), jnp.float32)
    signs, columns = shared_patterns(key)
    request_ids = jnp.arange(REQS, dtype=jnp.int32)
    pattern_index = request_ids // 4 % 3
    aligned = signs[pattern_index] * 3.0
    chosen = request_ids % 4 == 0
    first_row = jnp.where(chosen[:, None], aligned, values[:, 0, :])
    values = values.at[:, 0, :].set(first_row)
    return jnp.clip(values, -6.0, 6.0).astype(jnp.bfloat16)


def draw_hidden_policy(key, part):
    return hidden_matrix(key, 111)


def draw_hidden_reference(key, part):
    return hidden_matrix(key, 222)


def output_matrix(key, salt):
    base = jax.random.fold_in(key, salt)
    first = jax.random.fold_in(base, 0)
    values = jax.random.normal(first, (D, VOCAB), jnp.float32) * (3.0 / math.sqrt(D))
    signs, columns = shared_patterns(key)
    strengths = jnp.array([130.0, 128.0, 180.0, 177.5, 240.0, 238.0], jnp.float32)
    for index in range(6):
        column_values = signs[index // 2] * (strengths[index] / D)
        values = values.at[:, columns[index]].set(column_values)
    return jnp.clip(values, -4.0, 4.0).astype(jnp.bfloat16)


def draw_out_policy(key, part):
    return output_matrix(key, 101)


def draw_out_reference(key, part):
    return output_matrix(key, 202)


def draw_move_plan(key, part):
    base = jax.random.fold_in(key, 303)
    first, second, third = jax.random.split(base, 3)
    device_count = REQS // REQ_DEV
    offset_count = REQ_DEV // CAP
    half_way = device_count // 2
    others = jax.random.permutation(first, device_count - 2).astype(jnp.int32)
    others = others + (others >= 1).astype(jnp.int32)
    others = others + (others >= half_way).astype(jnp.int32)
    offsets = jnp.concatenate([jnp.full((1,), half_way, jnp.int32), jnp.ones((1,), jnp.int32), others[:offset_count - 2]])
    orders = jax.vmap(lambda item: jax.random.permutation(item, REQ_DEV))(jax.random.split(second, device_count))
    arrival = jax.random.permutation(third, REQ_DEV)
    group = orders // CAP
    copy_index = orders % CAP
    source = jnp.arange(device_count, dtype=jnp.int32)[:, None]
    owner = (source + offsets[group]) % device_count
    slot = arrival[group * CAP + copy_index]
    return (owner * REQ_DEV + slot).reshape(REQS).astype(jnp.int32)


def set_ends(entries, own_key, least, high):
    longest = entries.shape.index(max(entries.shape))
    spots = []
    for shift in (0, 1):
        where = [jax.random.randint(jax.random.fold_in(own_key, axis), (), 0, length) for axis, length in enumerate(entries.shape)]
        where[longest] = (where[longest] + shift) % entries.shape[longest]
        spots.append(tuple(where))
    return entries.at[spots[0]].set(least).at[spots[1]].set(high)


def raised(drawn, key, source, target, shards_of, factor):
    def block_of(dim):
        return (jnp.arange(drawn.shape[dim]) // (drawn.shape[dim] // shards_of)).reshape((-1,) + (1,) * (drawn.ndim - 1 - dim))

    first = jax.random.permutation(key, shards_of)[block_of(target)]
    other_side = (block_of(target) + shards_of // 2) % shards_of
    return jnp.where((block_of(source) == first) | (block_of(source) == other_side), factor * drawn, drawn)


def shard_levels(stream_key, dims, cuts, low, top_value):
    loudness, own = 1.0, jax.random.fold_in(stream_key, 6)
    for position, shards_of in cuts:
        steps = jnp.exp(jax.random.uniform(jax.random.fold_in(own, position), (shards_of,), jnp.float32, low / len(cuts), top_value / len(cuts)))
        loudness = loudness * jnp.repeat(steps, dims[position] // shards_of).reshape([-1 if axis == position else 1 for axis in range(len(dims))])
    return loudness


def rank_table(number_of, lean):
    weights = [(1 << 20) // math.isqrt(grade ** lean) + 1 for grade in range(1, number_of + 1)]
    deviation = 1 + sum(weights) // (1 << 30)
    return np.cumsum(np.array([max(1, weight // deviation) for weight in weights]))


def skewed_ids(stream_key, dims, count, slope):
    table = rank_table(count, slope)
    pick = jax.random.randint(jax.random.fold_in(stream_key, 1), dims, 0, int(table[count - 1]))
    standing = jnp.searchsorted(jnp.asarray(table, jnp.int32), pick, side="right")
    return jax.random.permutation(jax.random.fold_in(stream_key, 2), count)[standing].astype(jnp.int32)


def split_up(number_of, total, most, skew):
    portions = [(1 << 20) // math.isqrt(rank ** skew) + 1 for rank in range(2, number_of + 1)]
    rest, given = total - most - (number_of - 1), [1] * (number_of - 1)
    while rest > 0:
        candidates = [i for i in range(number_of - 1) if given[i] < most]
        pool, budget = sum([portions[i] for i in candidates]), rest
        for i in candidates:
            extra = min(most - given[i], max(1, budget * portions[i] // pool), rest)
            given[i] = given[i] + extra
            rest = rest - extra
    return np.array([most] + given)


def uneven_parts(key, count, total, reach, slope):
    if count == 2:
        one = jax.random.randint(key, (), max(1, total - reach), min(reach, total - 1) + 1)
        return jnp.stack([one, total - one])
    sizes = jnp.asarray(split_up(count, total, reach, slope), jnp.int32)
    twos = (count - 1) // 2
    source_of, sink = sizes[1:1 + 2 * twos:2], sizes[2:2 + 2 * twos:2]
    slack = jnp.minimum(source_of - 1, reach - sink)
    passed = jax.random.randint(jax.random.fold_in(key, 1), (twos,), 0, 1 << 20) % (slack + 1)
    sizes = sizes.at[1:1 + 2 * twos:2].set(source_of - passed).at[2:2 + 2 * twos:2].set(sink + passed)
    return sizes[jax.random.permutation(jax.random.fold_in(key, 2), count)]


def gaussian(stream_key, shape, width, reach, shards=(), kind=jnp.bfloat16):
    values = width * jax.random.normal(stream_key, shape, jnp.float32)
    if shards:
        values = values * shard_levels(stream_key, shape, shards, -0.22, 0.18)
    return jnp.clip(values, -reach, reach).astype(kind)


def noise_with(own_key, extent, deviation, bound, pieces, heavy, kind=jnp.bfloat16):
    values = deviation * jax.random.normal(own_key, extent, jnp.float32)
    if pieces:
        values = values * shard_levels(own_key, extent, pieces, -0.22, 0.18)
    return jnp.clip(raised(values, jax.random.fold_in(own_key, 3), *heavy), -bound, bound).astype(kind)


def setup_inputs(seed: int = 0) -> dict:
    key_of = jax.random.split(jax.random.key(seed), 16)
    hidden_policy = draw_hidden_policy(jax.random.fold_in(key_of[15], 71), 0)
    hidden_reference = draw_hidden_reference(jax.random.fold_in(key_of[15], 71), 0)
    ffn_gain_policy = jnp.clip(1.0 + 0.18 * jax.random.normal(key_of[2], (D,), jnp.float32), 0.1, 1.9)
    ffn_gain_reference = jnp.clip(1.0 + 0.18 * jax.random.normal(key_of[3], (D,), jnp.float32), 0.1, 1.9)
    up_policy = gaussian(key_of[4], (D, FF), D ** -0.5, 0.125, ((1, 32),))
    up_reference = gaussian(key_of[5], (D, FF), D ** -0.5, 0.125, ((1, 32),))
    down_policy = noise_with(key_of[6], (FF, D), FF ** -0.5, 0.1875, ((0, 32),), (0, 1, 32, 2.75))
    down_reference = noise_with(key_of[7], (FF, D), FF ** -0.5, 0.1875, ((0, 32),), (0, 1, 32, 2.75))
    final_gain_policy = jnp.clip(1.0 + 0.18 * jax.random.normal(key_of[8], (D,), jnp.float32), 0.1, 1.9)
    final_gain_reference = jnp.clip(1.0 + 0.18 * jax.random.normal(key_of[9], (D,), jnp.float32), 0.1, 1.9)
    out_policy = draw_out_policy(jax.random.fold_in(key_of[15], 71), 0)
    out_reference = draw_out_reference(jax.random.fold_in(key_of[15], 71), 0)
    move_plan = draw_move_plan(jax.random.fold_in(key_of[15], 71), 0)
    lengths = uneven_parts(key_of[13], REQS, REQS * SEQ // 2, SEQ, 2).astype(jnp.int32)
    targets = set_ends(skewed_ids(key_of[14], (REQS, SEQ), VOCAB, 2), jax.random.fold_in(key_of[14], 3), 0, VOCAB - 1).astype(jnp.int32)
    return {"hidden_policy": hidden_policy, "hidden_reference": hidden_reference, "ffn_gain_policy": ffn_gain_policy, "ffn_gain_reference": ffn_gain_reference, "up_policy": up_policy, "up_reference": up_reference, "down_policy": down_policy, "down_reference": down_reference, "final_gain_policy": final_gain_policy, "final_gain_reference": final_gain_reference, "out_policy": out_policy, "out_reference": out_reference, "move_plan": move_plan, "lengths": lengths, "targets": targets}


epsilon = 1e-05

def layer_norm(values, gain):
    center = lax.optimization_barrier(jnp.mean(values, axis=-1, keepdims=True))
    spread = lax.optimization_barrier(jnp.mean(jnp.square(values - center), axis=-1, keepdims=True))
    return (values - center) * lax.rsqrt(spread + epsilon) * gain

def model_logprob(hidden, move_plan, ffn_gain, up_weight, down_weight, final_gain, out_weight, target_flat):
    moved = jnp.zeros_like(hidden).at[move_plan].set(hidden)
    stream_in = moved.reshape(REQS * SEQ, D)
    normed_in = layer_norm(stream_in.astype(jnp.float32), ffn_gain).astype(jnp.bfloat16)
    pre = jnp.dot(normed_in, up_weight, preferred_element_type=jnp.float32)
    hidden_units = jax.nn.gelu(pre).astype(jnp.bfloat16)
    stream = stream_in.astype(jnp.float32) + jnp.dot(hidden_units, down_weight, preferred_element_type=jnp.float32)
    normed_out = layer_norm(stream, final_gain).astype(jnp.bfloat16)
    block = math.gcd(REQS * SEQ, 512)
    blocks = REQS * SEQ // block

    def score(pair):
        rows, wanted = pair
        logits = jnp.dot(rows, out_weight, preferred_element_type=jnp.float32)
        top = lax.optimization_barrier(jnp.max(logits, axis=1, keepdims=True))
        total = top[:, 0] + jnp.log(lax.optimization_barrier(jnp.sum(jnp.exp(logits - top), axis=1)))
        picked = jnp.take_along_axis(logits, wanted[:, None], axis=1)[:, 0]
        return picked - total
    scored = lax.map(score, (normed_out.reshape(blocks, block, D), target_flat.reshape(blocks, block)))
    return scored.reshape(REQS, SEQ)

def reference(hidden_policy, hidden_reference, ffn_gain_policy, ffn_gain_reference, up_policy, up_reference, down_policy, down_reference, final_gain_policy, final_gain_reference, out_policy, out_reference, move_plan, lengths, targets):
    target_flat = targets.reshape(REQS * SEQ).astype(jnp.int32)
    policy_lp = model_logprob(hidden_policy, move_plan, ffn_gain_policy, up_policy, down_policy, final_gain_policy, out_policy, target_flat)
    reference_lp = model_logprob(hidden_reference, move_plan, ffn_gain_reference, up_reference, down_reference, final_gain_reference, out_reference, target_flat)
    live = jnp.arange(SEQ, dtype=jnp.int32)[None, :] < lengths[:, None]
    token_diff = jnp.where(live, policy_lp - reference_lp, jnp.float32(0.0))
    seq_diff = lax.optimization_barrier(jnp.sum(token_diff, axis=1))
    return (token_diff, seq_diff)
```

```python
import functools

import jax
import jax.numpy as jnp
from jax import lax
from jax.experimental import pallas as pl
from jax.experimental.pallas import tpu as pltpu
from jax.sharding import PartitionSpec as P

MESH = pl.DeviceIdType.MESH
EPS = 1e-05
SIDE = 4
SUBS = 2
SUM_TYPE = jnp.float32
HIGH = lax.Precision.HIGHEST
f32 = jnp.float32
bf16 = jnp.bfloat16


def remote(src, dst, send_sem, recv_sem, device):
    return pltpu.make_async_remote_copy(
        src_ref=src,
        dst_ref=dst,
        send_sem=send_sem,
        recv_sem=recv_sem,
        device_id=device,
        device_id_type=MESH,
    )


def add_up(parts):
    while len(parts) > 1:
        parts = [
            parts[i] + parts[i + 1] if i + 1 < len(parts) else parts[i]
            for i in range(0, len(parts), 2)
        ]
    return parts[0]


def normed_tiles(tiles, gain, width):
    center = jnp.sum(add_up(tiles), axis=1, keepdims=True) / width
    tiles = [tile - center for tile in tiles]
    spread = jnp.sum(add_up([tile * tile for tile in tiles]), axis=1, keepdims=True) / width
    scale = lax.rsqrt(spread + EPS)
    return [
        (tile * scale * gain[:, i * 128 : (i + 1) * 128]).astype(bf16) for i, tile in enumerate(tiles)
    ]


def kernel(
    nz,
    hidden_p,
    hidden_r,
    ffn_gain_p,
    ffn_gain_r,
    up_p,
    up_r,
    down_p,
    down_r,
    final_gain_p,
    final_gain_r,
    out_p,
    out_r,
    plan_row,
    plan_cols,
    lengths,
    targets,
    token_diff,
    seq_diff,
    halves,
    feats,
    normed_in,
    up,
    down,
    out,
    partial,
    sums_out,
    sums_in,
    normed_out,
    logits,
    columns,
    wanted,
    target_col,
    select,
    stats,
    lane_lp,
    other_lp,
    diffs,
    local_sem,
    swap_send,
    swap_recv,
    gather_send,
    gather_recv,
    sum_send,
    sum_recv,
    spread_send,
    spread_recv,
    near_send,
    near_recv,
    far_send,
    far_recv,
    target_send,
    target_recv,
    stat_send,
    stat_recv,
    pair_send,
    pair_recv,
    diff_send,
    diff_recv,
):
    dp = lax.axis_index("dp")
    mp = lax.axis_index("mp")
    z, core = mp // 2, mp % 2
    x, y = dp // SIDE, dp % SIDE
    ndp = SIDE * SIDE
    tokens, width = normed_out.shape
    nfeat = width // 128
    own_tokens = tokens // nz
    units = up_p.shape[1]
    vocab = out_p.shape[1]
    depth = out_p.shape[0]
    piece = depth // 2
    quarter = piece // 2
    waits = []

    def z_peer(step):
        return (dp, ((z + step + nz) % nz) * 2 + core)

    def xy_peer(axis, step):
        if axis == 0:
            return (((x + step + SIDE) % SIDE) * SIDE + y, mp)
        return (x * SIDE + (y + step + SIDE) % SIDE, mp)

    sibling = (dp, z * 2 + 1 - core)

    def send(copy):
        copy.start()
        waits.append(copy)

    barrier = pltpu.get_barrier_semaphore()
    greeted = [sibling, z_peer(1), z_peer(-1)]
    greeted += [xy_peer(axis, step) for axis in (0, 1) for step in (1, -1)]
    for device in greeted:
        pl.semaphore_signal(barrier, inc=1, device_id=device, device_id_type=MESH)
    pl.semaphore_wait(barrier, len(greeted))

    own_rows = pl.ds(pl.multiple_of(dp * depth, depth), depth)

    def places(c):
        return (
            halves.at[c],
            out.at[own_rows, c * vocab : (c + 1) * vocab],
            up.at[:, c * units : (c + 1) * units],
            down.at[c * units : (c + 1) * units, :],
        )

    policy = (hidden_p, out_p, up_p, down_p)
    refer = (hidden_r, out_r, up_r, down_r)
    for c in (0, 1):

        @pl.when(core == c)
        def _(c=c):
            mine, theirs = (policy, refer) if c == 0 else (refer, policy)
            for i, place in enumerate(places(c)):
                remote(theirs[i], place, swap_send.at[i], swap_recv.at[i], sibling).start()
                pltpu.make_async_copy(mine[i], place, local_sem.at[i]).start()

    def swap_wait(i):
        for c in (0, 1):

            @pl.when(core == c)
            def _(c=c):
                mine, theirs = (policy, refer) if c == 0 else (refer, policy)
                remote(
                    theirs[i], places(1 - c)[i], swap_send.at[i], swap_recv.at[i], sibling
                ).wait_recv()
                pltpu.make_async_copy(mine[i], places(c)[i], local_sem.at[i]).wait()

    def swap_done(i):
        for c in (0, 1):

            @pl.when(core == c)
            def _(c=c):
                theirs = refer if c == 0 else policy
                remote(
                    theirs[i], places(c)[i], swap_send.at[i], swap_recv.at[i], sibling
                ).wait_send()

    plus, minus = nz // 2, nz // 2 - 1

    def ring_gather(block, send_sem, recv_sem, hooks):
        for k in range(plus + 1):
            for sub in range(SUBS):
                for way, hops, step in ((0, plus, 1), (1, minus, -1)):
                    if 1 <= k <= hops:
                        arrived = block((z - step * k + nz) % nz, sub)
                        remote(
                            arrived,
                            arrived,
                            send_sem.at[way, k - 1, sub],
                            recv_sem.at[way, k - 1, sub],
                            z_peer(step),
                        ).wait_recv()
                    if k < hops:
                        held = block((z - step * k + nz) % nz, sub)
                        send(
                            remote(
                                held,
                                held,
                                send_sem.at[way, k, sub],
                                recv_sem.at[way, k, sub],
                                z_peer(step),
                            )
                        )
            if k in hooks:
                hooks[k]()

    def block_rows(h, along, across, part):
        first, second = (along, across) if h == 0 else (across, along)
        start = (first * SIDE + second) * depth + h * piece
        if part is None:
            return out.at[pl.ds(pl.multiple_of(start, piece), piece), :]
        return out.at[pl.ds(pl.multiple_of(start + part * quarter, quarter), quarter), :]

    def place_of(h):
        return (x, y) if h == 0 else (y, x)

    def along_of(h, j):
        return (place_of(h)[0] + (0, -1, 1, 2)[j] + SIDE) % SIDE

    def near(h, way, forward):
        step = (1, -1)[way]
        u, v = place_of(h)
        if forward:
            rows = block_rows(h, (u - step + SIDE) % SIDE, v, way)
        else:
            rows = block_rows(h, u, v, None)
        sem = (h, way, int(forward))
        return remote(rows, rows, near_send.at[sem], near_recv.at[sem], xy_peer(h, step))

    def near_wait(h, way, forward):
        step = (1, -1)[way]
        u, v = place_of(h)
        if forward:
            rows = block_rows(h, (u - 2 * step + SIDE) % SIDE, v, way)
        else:
            rows = block_rows(h, (u - step + SIDE) % SIDE, v, None)
        sem = (h, way, int(forward))
        remote(rows, rows, near_send.at[sem], near_recv.at[sem], xy_peer(h, step)).wait_recv()

    def far(h, j, way, forward):
        step = (1, -1)[way]
        v = place_of(h)[1]
        if forward:
            rows = block_rows(h, along_of(h, j), (v - step + SIDE) % SIDE, way)
        else:
            rows = block_rows(h, along_of(h, j), v, None)
        sem = (h, j, way, int(forward))
        return remote(rows, rows, far_send.at[sem], far_recv.at[sem], xy_peer(1 - h, step))

    def far_wait(h, j, way, forward):
        step = (1, -1)[way]
        v = place_of(h)[1]
        if forward:
            rows = block_rows(h, along_of(h, j), (v - 2 * step + SIDE) % SIDE, way)
        else:
            rows = block_rows(h, along_of(h, j), (v - step + SIDE) % SIDE, None)
        sem = (h, j, way, int(forward))
        remote(rows, rows, far_send.at[sem], far_recv.at[sem], xy_peer(1 - h, step)).wait_recv()

    both = [(h, way) for h in (0, 1) for way in (0, 1)]

    def out_round_0():
        swap_wait(1)
        for h, way in both:
            send(near(h, way, False))
        for h, way in both:
            send(far(h, 0, way, False))

    def out_round_1():
        for h, way in both:
            near_wait(h, way, False)
            send(near(h, way, True))
        for j in (1, 2):
            for h, way in both:
                send(far(h, j, way, False))
        for h, way in both:
            far_wait(h, 0, way, False)
            send(far(h, 0, way, True))

    def out_round_2():
        for h, way in both:
            near_wait(h, way, True)
        for h, way in both:
            send(far(h, 3, way, False))
        for j in (1, 2):
            for h, way in both:
                far_wait(h, j, way, False)
                send(far(h, j, way, True))

    def out_round_3():
        for h, way in both:
            far_wait(h, 3, way, False)
            send(far(h, 3, way, True))

    def out_round_4():
        for j in range(4):
            for h, way in both:
                far_wait(h, j, way, True)

    swap_wait(0)
    feats[z] = jnp.concatenate([halves[0], halves[1]], axis=1)
    sub_tokens = tokens // SUBS

    def feat_block(source, sub):
        return feats.at[source, sub * sub_tokens : (sub + 1) * sub_tokens, :]

    ring_gather(
        feat_block, gather_send, gather_recv, {0: out_round_0, min(6, plus): out_round_1}
    )

    first_gain = jnp.where(core == 0, ffn_gain_p[...], ffn_gain_r[...])
    row_step = 16

    @pl.loop(0, tokens // row_step)
    def _(i):
        rows = pl.ds(pl.multiple_of(i * row_step, row_step), row_step)
        tiles = [feats[k, rows, :].astype(f32) for k in range(nfeat)]
        for k, tile in enumerate(normed_tiles(tiles, first_gain, width)):
            normed_in[rows, k * 128 : (k + 1) * 128] = tile

    swap_wait(2)
    swap_wait(3)
    pre = jnp.dot(normed_in[...], up[...], preferred_element_type=f32)
    active = jax.nn.gelu(pre).astype(bf16)
    partial[...] = jnp.dot(active, down[...], preferred_element_type=f32)

    sub_width = width // SUBS

    def rows_of(chunk):
        return pl.ds(pl.multiple_of(chunk * own_tokens, own_tokens), own_tokens)

    def sum_copy(way, s, sub):
        cols = slice(sub * sub_width, (sub + 1) * sub_width)
        return remote(
            sums_out.at[way, s, :, cols],
            sums_in.at[way, s, :, cols],
            sum_send.at[way, s, sub],
            sum_recv.at[way, s, sub],
            z_peer((1, -1)[way]),
        )

    sum_hooks = {min(4, plus - 1): out_round_2, plus - 1: out_round_3}
    for s in range(plus):
        for sub in range(SUBS):
            cols = slice(sub * sub_width, (sub + 1) * sub_width)
            for way, hops, step in ((0, plus, 1), (1, minus, -1)):
                if s >= hops:
                    continue
                rows = rows_of((z + step * (hops - s) + nz) % nz)
                term = partial[rows, cols]
                if s > 0:
                    sum_copy(way, s - 1, sub).wait_recv()
                    term = term + sums_in[way, s - 1, :, cols].astype(f32)
                sums_out[way, s, :, cols] = term.astype(sums_out.dtype)
                send(sum_copy(way, s, sub))
        if s in sum_hooks:
            sum_hooks[s]()
    for sub in range(SUBS):
        sum_copy(0, plus - 1, sub).wait_recv()
        sum_copy(1, minus - 1, sub).wait_recv()

    second_gain = jnp.where(core == 0, final_gain_p[...], final_gain_r[...])
    mine = rows_of(z)
    tiles = []
    for k in range(nfeat):
        cols = slice(k * 128, (k + 1) * 128)
        total = (
            partial[mine, cols]
            + sums_in[0, plus - 1, :, cols].astype(f32)
            + sums_in[1, minus - 1, :, cols].astype(f32)
        )
        tiles.append(feats[k, mine, :].astype(f32) + total)
    for k, tile in enumerate(normed_tiles(tiles, second_gain, width)):
        normed_out[mine, k * 128 : (k + 1) * 128] = tile

    def out_block(source, sub):
        return normed_out.at[rows_of(source), sub * sub_width : (sub + 1) * sub_width]

    ring_gather(out_block, spread_send, spread_recv, {})
    out_round_4()

    wanted[dp] = targets[...]

    def target_copy(i):
        return remote(
            wanted.at[dp], wanted.at[dp], target_send.at[i], target_recv.at[i], ((dp + i) % ndp, mp)
        )

    for i in range(1, ndp):
        send(target_copy(i))

    block = 256

    @pl.loop(0, 2 * vocab // block)
    def _(i):
        cols = pl.ds(pl.multiple_of(i * block, block), block)
        logits[:, cols] = jnp.dot(normed_out[...], out[:, cols], preferred_element_type=f32)

    slots = plan_cols.shape[0]
    seq = targets.shape[1]
    for i in range(1, ndp):
        place = wanted.at[(dp - i + ndp) % ndp]
        remote(place, place, target_send.at[i], target_recv.at[i], ((dp + i) % ndp, mp)).wait_recv()
    token = lax.broadcasted_iota(jnp.int32, (tokens, ndp * slots), 0)
    lane = lax.broadcasted_iota(jnp.int32, (tokens, ndp * slots), 1)
    own_request = lane == dp * slots + token // seq
    owner_slot = jnp.sum(
        jnp.where(own_request, plan_row[...].astype(f32), 0.0), axis=1, keepdims=True
    )
    slot_hot = jnp.where(lane.astype(f32) == owner_slot, 1.0, 0.0)
    all_targets = wanted[...].astype(f32).reshape(ndp * slots, seq)
    seen = jnp.dot(slot_hot, all_targets, precision=HIGH, preferred_element_type=f32)
    position = lax.broadcasted_iota(jnp.int32, (tokens, seq), 1)
    row = lax.broadcasted_iota(jnp.int32, (tokens, seq), 0)
    target_col[...] = jnp.sum(
        jnp.where(position == row % seq, seen, 0.0), axis=1, keepdims=True
    ).astype(jnp.int32)

    plan = plan_cols[...]
    slot_id = lax.broadcasted_iota(jnp.int32, (slots, slots, ndp), 1) + dp * slots
    hot = jnp.broadcast_to(plan[:, None, :], (slots, slots, ndp)) == slot_id
    select[...] = jnp.where(hot, 1.0, 0.0).reshape(slots * slots, ndp)

    ntile = 2 * vocab // 128

    @pl.loop(0, tokens // row_step)
    def _(i):
        rows = pl.ds(pl.multiple_of(i * row_step, row_step), row_step)
        tiles = [logits[rows, k * 128 : (k + 1) * 128] for k in range(ntile)]
        top = tiles[0]
        for tile in tiles[1:]:
            top = jnp.maximum(top, tile)
        top = jnp.max(top, axis=1, keepdims=True)
        total = jnp.sum(add_up([jnp.exp(tile - top) for tile in tiles]), axis=1, keepdims=True)
        place = lax.broadcasted_iota(jnp.int32, (row_step, 128), 1)
        spot = target_col[rows, :] - z * (2 * vocab)
        hits = add_up(
            [jnp.where(place == spot - k * 128, tile, 0.0) for k, tile in enumerate(tiles)]
        )
        picked = jnp.sum(hits, axis=1, keepdims=True)
        local = top + jnp.log(total)
        columns[rows, :] = jnp.where(place == 0, local, jnp.where(place == 1, picked, 0.0))

    turned = columns[...].T
    ngroup = tokens // 128
    for g in range(ngroup):
        stats[z, g : g + 1, :] = turned[0:1, g * 128 : (g + 1) * 128]
        stats[z, ngroup + g : ngroup + g + 1, :] = turned[1:2, g * 128 : (g + 1) * 128]

    for i in range(1, nz):
        send(remote(stats.at[z], stats.at[z], stat_send.at[i], stat_recv.at[i], z_peer(i)))
    for i in range(1, nz):
        place = stats.at[(z - i + nz) % nz]
        remote(place, place, stat_send.at[i], stat_recv.at[i], z_peer(i)).wait_recv()
    parts = [stats[i] for i in range(nz)]
    sums = [part[:ngroup] for part in parts]
    top = sums[0]
    for part in sums[1:]:
        top = jnp.maximum(top, part)
    total = add_up([jnp.exp(part - top) for part in sums])
    picked = add_up([part[ngroup:] for part in parts])
    lane_lp[...] = picked - (top + jnp.log(total))

    swap = remote(lane_lp, other_lp, pair_send, pair_recv, sibling)
    send(swap)
    swap.wait_recv()
    difference = jnp.where(
        core == 0, lane_lp[...] - other_lp[...], other_lp[...] - lane_lp[...]
    )
    diffs[dp] = difference

    for i in range(1, ndp):
        send(
            remote(
                diffs.at[dp], diffs.at[dp], diff_send.at[i], diff_recv.at[i], ((dp + i) % ndp, mp)
            )
        )
    for i in range(1, ndp):
        place = diffs.at[(dp - i + ndp) % ndp]
        remote(place, place, diff_send.at[i], diff_recv.at[i], ((dp + i) % ndp, mp)).wait_recv()

    per_group = slots // ngroup
    taken = []
    for g in range(ngroup):
        hot = select[g * per_group * slots : (g + 1) * per_group * slots, :]
        got = jnp.dot(hot, diffs[:, g, :], precision=HIGH, preferred_element_type=f32)
        row = lax.broadcasted_iota(jnp.int32, got.shape, 0) // slots
        lane = lax.broadcasted_iota(jnp.int32, got.shape, 1) // seq
        got = jnp.where(row == lane, got, 0.0)
        taken += [got[j * slots : (j + 1) * slots] for j in range(per_group)]
    fold = jnp.where(
        lax.broadcasted_iota(jnp.int32, (128, seq), 0) % seq
        == lax.broadcasted_iota(jnp.int32, (128, seq), 1),
        1.0,
        0.0,
    )
    moved = jnp.dot(add_up(taken), fold, precision=HIGH, preferred_element_type=f32)
    live = lax.broadcasted_iota(jnp.int32, (slots, seq), 1) < lengths[...]
    kept = jnp.where(live, moved, 0.0)
    token_diff[...] = kept
    seq_diff[...] = jnp.sum(kept, axis=1, keepdims=True)

    for i in range(4):
        swap_done(i)
    for copy in waits:
        copy.wait_send()


def local(
    nz,
    hidden_policy,
    hidden_reference,
    ffn_gain_policy,
    ffn_gain_reference,
    up_policy,
    up_reference,
    down_policy,
    down_reference,
    final_gain_policy,
    final_gain_reference,
    out_policy,
    out_reference,
    move_plan,
    lengths,
    targets,
):
    slots, seq, part = hidden_policy.shape
    tokens = slots * seq
    width = up_policy.shape[0]
    units = up_policy.shape[1]
    vocab = out_policy.shape[1]
    ndp = SIDE * SIDE
    own = tokens // nz
    ngroup = tokens // 128
    plus = nz // 2
    any_space = pl.BlockSpec(memory_space=pl.ANY)
    vmem = pl.BlockSpec(memory_space=pltpu.VMEM)
    dma = pltpu.SemaphoreType.DMA
    ring = (2, plus, SUBS)
    token_diff, seq_diff = pl.pallas_call(
        functools.partial(kernel, nz),
        out_shape=(
            jax.ShapeDtypeStruct((slots, seq), f32),
            jax.ShapeDtypeStruct((slots, 1), f32),
        ),
        in_specs=[any_space, any_space, vmem, vmem]
        + [any_space] * 4
        + [vmem, vmem, any_space, any_space]
        + [vmem] * 4,
        out_specs=(vmem, vmem),
        scratch_shapes=[
            pltpu.VMEM((2, tokens, part), bf16),
            pltpu.VMEM((width // 128, tokens, 128), bf16),
            pltpu.VMEM((tokens, width), bf16),
            pltpu.VMEM((width, 2 * units), bf16),
            pltpu.VMEM((2 * units, width), bf16),
            pltpu.VMEM((width, 2 * vocab), bf16),
            pltpu.VMEM((tokens, width), f32),
            pltpu.VMEM((2, plus, own, width), SUM_TYPE),
            pltpu.VMEM((2, plus, own, width), SUM_TYPE),
            pltpu.VMEM((tokens, width), bf16),
            pltpu.VMEM((tokens, 2 * vocab), f32),
            pltpu.VMEM((tokens, 128), f32),
            pltpu.VMEM((ndp, slots, seq), jnp.int32),
            pltpu.VMEM((tokens, 1), jnp.int32),
            pltpu.VMEM((slots * slots, ndp), f32),
            pltpu.VMEM((nz, 2 * ngroup, 128), f32),
            pltpu.VMEM((ngroup, 128), f32),
            pltpu.VMEM((ngroup, 128), f32),
            pltpu.VMEM((ndp, ngroup, 128), f32),
            dma((4,)),
            dma((4,)),
            dma((4,)),
            dma(ring),
            dma(ring),
            dma(ring),
            dma(ring),
            dma(ring),
            dma(ring),
            dma((2, 2, 2)),
            dma((2, 2, 2)),
            dma((2, 4, 2, 2)),
            dma((2, 4, 2, 2)),
            dma((ndp,)),
            dma((ndp,)),
            dma((nz,)),
            dma((nz,)),
            dma,
            dma,
            dma((ndp,)),
            dma((ndp,)),
        ],
        compiler_params=pltpu.CompilerParams(
            collective_id=0, has_side_effects=True, vmem_limit_bytes=48 * 1024 * 1024
        ),
        name="score",
    )(
        hidden_policy.reshape(tokens, part),
        hidden_reference.reshape(tokens, part),
        ffn_gain_policy.reshape(1, width),
        ffn_gain_reference.reshape(1, width),
        up_policy,
        up_reference,
        down_policy,
        down_reference,
        final_gain_policy.reshape(1, width),
        final_gain_reference.reshape(1, width),
        out_policy,
        out_reference,
        move_plan.reshape(1, ndp * slots),
        move_plan.reshape(ndp, slots).T,
        lengths.reshape(slots, 1),
        targets,
    )
    return token_diff, seq_diff.reshape(slots)


def solution(mesh):
    nz = mesh.shape["mp"] // 2
    return jax.shard_map(
        functools.partial(local, nz),
        mesh=mesh,
        in_specs=(
            P("dp", None, "mp"),
            P("dp", None, "mp"),
            P(),
            P(),
            P(None, "mp"),
            P(None, "mp"),
            P("mp", None),
            P("mp", None),
            P(),
            P(),
            P("dp", "mp"),
            P("dp", "mp"),
            P(),
            P("dp"),
            P("dp", None),
        ),
        out_specs=(P("dp", None), P("dp")),
        check_vma=False,
    )
```

```python
import functools

import jax
import jax.numpy as jnp
from jax import lax
from jax.experimental import pallas as pl
from jax.experimental.pallas import tpu as pltpu
from jax.sharding import PartitionSpec as P

MESH = pl.DeviceIdType.MESH
EPS = 1e-05
SIDE = 4
SUBS = 2
SUM_TYPE = jnp.bfloat16
HIGH = lax.Precision.HIGHEST
f32 = jnp.float32
bf16 = jnp.bfloat16


def remote(src, dst, send_sem, recv_sem, device):
    return pltpu.make_async_remote_copy(
        src_ref=src,
        dst_ref=dst,
        send_sem=send_sem,
        recv_sem=recv_sem,
        device_id=device,
        device_id_type=MESH,
    )


def add_up(parts):
    while len(parts) > 1:
        parts = [
            parts[i] + parts[i + 1] if i + 1 < len(parts) else parts[i]
            for i in range(0, len(parts), 2)
        ]
    return parts[0]


def normed_tiles(load, count, gain, width, store):
    center = jnp.sum(add_up([load(i) for i in range(count)]), axis=1, keepdims=True) / width
    squares = [jnp.square(load(i) - center) for i in range(count)]
    spread = jnp.sum(add_up(squares), axis=1, keepdims=True) / width
    scale = lax.rsqrt(spread + EPS)
    for i in range(count):
        tile = (load(i) - center) * scale * gain[:, i * 128 : (i + 1) * 128]
        store(i, tile.astype(bf16))


def kernel(
    nz,
    hidden_p,
    hidden_r,
    ffn_gain_p,
    ffn_gain_r,
    up_p,
    up_r,
    down_p,
    down_r,
    final_gain_p,
    final_gain_r,
    out_p,
    out_r,
    plan_hbm,
    lengths_hbm,
    targets,
    token_diff,
    seq_diff,
    plan_row,
    lengths,
    gains,
    after,
    halves,
    feats,
    normed_in,
    up,
    down,
    out,
    partial,
    sums_out,
    sums_in,
    normed_out,
    logits,
    columns,
    wanted,
    target_col,
    slot_hot,
    select,
    stats,
    lane_lp,
    other_lp,
    diffs,
    local_sem,
    swap_send,
    swap_recv,
    gather_send,
    gather_recv,
    sum_send,
    sum_recv,
    spread_send,
    spread_recv,
    near_send,
    near_recv,
    far_send,
    far_recv,
    target_send,
    target_recv,
    stat_send,
    stat_recv,
    pair_send,
    pair_recv,
    diff_send,
    diff_recv,
):
    dp = lax.axis_index("dp")
    mp = lax.axis_index("mp")
    z, core = mp // 2, mp % 2
    x, y = dp // SIDE, dp % SIDE
    ndp = SIDE * SIDE
    tokens, width = normed_out.shape
    slots, seq = token_diff.shape
    nfeat = width // 128
    own_tokens = tokens // nz
    units = up_p.shape[1]
    vocab = out_p.shape[1]
    depth = out_p.shape[0]
    piece = depth // 2
    quarter = piece // 2
    waits = []

    def z_peer(step):
        return (dp, ((z + step + nz) % nz) * 2 + core)

    def xy_peer(axis, step):
        if axis == 0:
            return (((x + step + SIDE) % SIDE) * SIDE + y, mp)
        return (x * SIDE + (y + step + SIDE) % SIDE, mp)

    sibling = (dp, z * 2 + 1 - core)

    def send(copy):
        copy.start()
        waits.append(copy)

    own_rows = pl.ds(pl.multiple_of(dp * depth, depth), depth)

    def places(c):
        return (
            halves.at[c],
            out.at[own_rows, c * vocab : (c + 1) * vocab],
            up.at[:, c * units : (c + 1) * units],
            down.at[c * units : (c + 1) * units, :],
        )

    policy = (hidden_p, out_p, up_p, down_p, ffn_gain_p, final_gain_p)
    refer = (hidden_r, out_r, up_r, down_r, ffn_gain_r, final_gain_r)

    def local_copy(c, i):
        mine = policy if c == 0 else refer
        place = gains.at[i - 4] if i >= 4 else places(c)[i]
        return pltpu.make_async_copy(mine[i], place, local_sem.at[i])

    small_copies = [
        pltpu.make_async_copy(plan_hbm, plan_row, local_sem.at[6]),
        pltpu.make_async_copy(lengths_hbm, lengths, local_sem.at[7]),
        pltpu.make_async_copy(targets, wanted.at[dp], local_sem.at[8]),
    ]
    for c in (0, 1):

        @pl.when(core == c)
        def _(c=c):
            for i in range(6):
                local_copy(c, i).start()

    for copy in small_copies:
        copy.start()

    barrier = pltpu.get_barrier_semaphore()
    greeted = [sibling] + [z_peer(step) for step in (1, -1, 2, -2)]
    greeted += [xy_peer(axis, step) for axis in (0, 1) for step in (1, -1)]
    for device in greeted:
        pl.semaphore_signal(barrier, inc=1, device_id=device, device_id_type=MESH)
    pl.semaphore_wait(barrier, len(greeted))

    for c in (0, 1):

        @pl.when(core == c)
        def _(c=c):
            theirs = refer if c == 0 else policy
            for i, place in enumerate(places(c)):
                remote(theirs[i], place, swap_send.at[i], swap_recv.at[i], sibling).start()

    def swap_wait(i):
        for c in (0, 1):

            @pl.when(core == c)
            def _(c=c):
                theirs = refer if c == 0 else policy
                remote(
                    theirs[i], places(1 - c)[i], swap_send.at[i], swap_recv.at[i], sibling
                ).wait_recv()
                local_copy(c, i).wait()

    def swap_done(i):
        for c in (0, 1):

            @pl.when(core == c)
            def _(c=c):
                theirs = refer if c == 0 else policy
                remote(
                    theirs[i], places(c)[i], swap_send.at[i], swap_recv.at[i], sibling
                ).wait_send()

    plus, minus = nz // 2, nz // 2 - 1

    ways = ((0, plus, 1), (1, minus, -1))

    def tree_gather(block, send_sem, recv_sem, hooks):
        def copy(way, step, t, sub, held, far):
            return remote(
                block((z - step * held + nz) % nz, sub),
                block((z - step * held + nz) % nz, sub),
                send_sem.at[way, t - 1, sub],
                recv_sem.at[way, t - 1, sub],
                z_peer(step * far),
            )

        for held in range(0, plus + 1, 2):
            for sub in range(SUBS):
                for way, hops, step in ways:
                    if 0 < held <= hops:
                        copy(way, step, held, sub, held, 2).wait_recv()
                    for far in (2, 1):
                        if held + far <= hops:
                            send(copy(way, step, held + far, sub, held, far))
            if held in hooks:
                hooks[held]()
        for t in range(1, plus + 1, 2):
            for sub in range(SUBS):
                for way, hops, step in ways:
                    if t <= hops:
                        copy(way, step, t, sub, t, 1).wait_recv()

    def block_rows(h, along, across, part):
        first, second = (along, across) if h == 0 else (across, along)
        start = (first * SIDE + second) * depth + h * piece
        if part is None:
            return out.at[pl.ds(pl.multiple_of(start, piece), piece), :]
        return out.at[pl.ds(pl.multiple_of(start + part * quarter, quarter), quarter), :]

    def place_of(h):
        return (x, y) if h == 0 else (y, x)

    def along_of(h, j):
        return (place_of(h)[0] + (0, -1, 1, 2)[j] + SIDE) % SIDE

    def near(h, way, forward):
        step = (1, -1)[way]
        u, v = place_of(h)
        if forward:
            rows = block_rows(h, (u - step + SIDE) % SIDE, v, way)
        else:
            rows = block_rows(h, u, v, None)
        sem = (h, way, int(forward))
        return remote(rows, rows, near_send.at[sem], near_recv.at[sem], xy_peer(h, step))

    def near_wait(h, way, forward):
        step = (1, -1)[way]
        u, v = place_of(h)
        if forward:
            rows = block_rows(h, (u - 2 * step + SIDE) % SIDE, v, way)
        else:
            rows = block_rows(h, (u - step + SIDE) % SIDE, v, None)
        sem = (h, way, int(forward))
        remote(rows, rows, near_send.at[sem], near_recv.at[sem], xy_peer(h, step)).wait_recv()

    def far(h, j, way, forward):
        step = (1, -1)[way]
        v = place_of(h)[1]
        if forward:
            rows = block_rows(h, along_of(h, j), (v - step + SIDE) % SIDE, way)
        else:
            rows = block_rows(h, along_of(h, j), v, None)
        sem = (h, j, way, int(forward))
        return remote(rows, rows, far_send.at[sem], far_recv.at[sem], xy_peer(1 - h, step))

    def far_wait(h, j, way, forward):
        step = (1, -1)[way]
        v = place_of(h)[1]
        if forward:
            rows = block_rows(h, along_of(h, j), (v - 2 * step + SIDE) % SIDE, way)
        else:
            rows = block_rows(h, along_of(h, j), (v - step + SIDE) % SIDE, None)
        sem = (h, j, way, int(forward))
        remote(rows, rows, far_send.at[sem], far_recv.at[sem], xy_peer(1 - h, step)).wait_recv()

    both = [(h, way) for h in (0, 1) for way in (0, 1)]

    def out_round_0():
        swap_wait(1)
        for h, way in both:
            send(near(h, way, False))
        for h, way in both:
            send(far(h, 0, way, False))

    def out_round_1():
        for h, way in both:
            near_wait(h, way, False)
            send(near(h, way, True))
        for j in (1, 2):
            for h, way in both:
                send(far(h, j, way, False))
        for h, way in both:
            far_wait(h, 0, way, False)
            send(far(h, 0, way, True))

    def out_round_2():
        for h, way in both:
            near_wait(h, way, True)
        for h, way in both:
            send(far(h, 3, way, False))
        for j in (1, 2):
            for h, way in both:
                far_wait(h, j, way, False)
                send(far(h, j, way, True))

    def out_round_3():
        for h, way in both:
            far_wait(h, 3, way, False)
            send(far(h, 3, way, True))

    def out_round_4():
        for j in range(4):
            for h, way in both:
                far_wait(h, j, way, True)

    swap_wait(0)
    feats[z] = jnp.concatenate([halves[0], halves[1]], axis=1)
    sub_tokens = tokens // SUBS

    def feat_block(source, sub):
        return feats.at[source, sub * sub_tokens : (sub + 1) * sub_tokens, :]

    def index_work():
        for copy in small_copies:
            copy.wait()
        request = lax.broadcasted_iota(jnp.int32, (slots, ndp * slots), 1)
        order = lax.broadcasted_iota(jnp.int32, (slots, ndp * slots), 0)
        spread_plan = jnp.where(request % slots == order, plan_row[...], 0).astype(bf16)
        request = lax.broadcasted_iota(jnp.int32, (ndp * slots, ndp), 0)
        holder = lax.broadcasted_iota(jnp.int32, (ndp * slots, ndp), 1)
        owner = jnp.where(request // slots == holder, 1.0, 0.0).astype(bf16)
        plan = jnp.dot(spread_plan, owner, preferred_element_type=f32)
        slot_id = lax.broadcasted_iota(jnp.int32, (slots, slots, ndp), 1) + dp * slots
        hot = jnp.broadcast_to(plan[:, None, :], (slots, slots, ndp)) == slot_id.astype(f32)
        select[...] = jnp.where(hot, 1.0, 0.0).reshape(slots * slots, ndp)
        token = lax.broadcasted_iota(jnp.int32, (tokens, ndp * slots), 0)
        lane = lax.broadcasted_iota(jnp.int32, (tokens, ndp * slots), 1)
        own_request = lane == dp * slots + token // seq
        owner_slot = jnp.sum(
            jnp.where(own_request, plan_row[...].astype(f32), 0.0), axis=1, keepdims=True
        )
        slot_hot[...] = jnp.where(lane.astype(f32) == owner_slot, 1.0, 0.0)

    def first_hook():
        out_round_0()
        index_work()

    tree_gather(feat_block, gather_send, gather_recv, {0: first_hook, 4: out_round_1})

    for i in (4, 5):
        for c in (0, 1):

            @pl.when(core == c)
            def _(c=c, i=i):
                local_copy(c, i).wait()

    row_step = min(64, tokens)

    @pl.loop(0, tokens // row_step)
    def _(i):
        rows = pl.ds(pl.multiple_of(i * row_step, row_step), row_step)

        def store(k, tile):
            normed_in[rows, k * 128 : (k + 1) * 128] = tile

        normed_tiles(lambda k: feats[k, rows, :].astype(f32), nfeat, gains[0], width, store)

    swap_wait(2)
    swap_wait(3)
    pre = jnp.dot(normed_in[...], up[...], preferred_element_type=f32)
    active = jax.nn.gelu(pre).astype(bf16)
    partial[...] = jnp.dot(active, down[...], preferred_element_type=f32)

    sub_width = width // SUBS

    def rows_of(chunk):
        return pl.ds(pl.multiple_of(chunk * own_tokens, own_tokens), own_tokens)

    def sum_copy(way, t, sub):
        cols = slice(sub * sub_width, (sub + 1) * sub_width)
        return remote(
            sums_out.at[way, t - 1, :, cols],
            sums_in.at[way, t - 1, :, cols],
            sum_send.at[way, t - 1, sub],
            sum_recv.at[way, t - 1, sub],
            z_peer((1, -1)[way] * (1 if t % 2 else 2)),
        )

    def hand_on(t):
        for sub in range(SUBS):
            cols = slice(sub * sub_width, (sub + 1) * sub_width)
            for way, hops, step in ways:
                if t > hops:
                    continue
                term = partial[rows_of((z + step * t + nz) % nz), cols]
                if t % 2 == 0:
                    for behind in (t + 2, t + 1):
                        if behind <= hops:
                            sum_copy(way, behind, sub).wait_recv()
                            term = term + sums_in[way, behind - 1, :, cols].astype(f32)
                sums_out[way, t - 1, :, cols] = term.astype(sums_out.dtype)
                send(sum_copy(way, t, sub))

    hand_on(plus)
    hand_on(plus - 1)
    for t in range(plus - 2, 0, -2):
        hand_on(t - 1)
        hand_on(t)
        if t == plus - 2:
            out_round_2()
    out_round_3()
    for t in (1, 2):
        for sub in range(SUBS):
            for way in (0, 1):
                sum_copy(way, t, sub).wait_recv()

    mine = rows_of(z)
    for k in range(nfeat):
        cols = slice(k * 128, (k + 1) * 128)
        came = [sums_in[way, t, :, cols].astype(f32) for way in (0, 1) for t in (0, 1)]
        total = partial[mine, cols] + add_up(came)
        after[k] = feats[k, mine, :].astype(f32) + total

    def store_out(k, tile):
        normed_out[mine, k * 128 : (k + 1) * 128] = tile

    normed_tiles(lambda k: after[k], nfeat, gains[1], width, store_out)

    def out_block(source, sub):
        return normed_out.at[rows_of(source), sub * sub_width : (sub + 1) * sub_width]

    def target_copy(i, source):
        return remote(
            wanted.at[source],
            wanted.at[source],
            target_send.at[i],
            target_recv.at[i],
            ((dp + i) % ndp, mp),
        )

    def send_targets():
        out_round_4()
        for i in range(1, ndp):
            send(target_copy(i, dp))

    def target_work():
        for i in range(1, ndp):
            target_copy(i, (dp - i + ndp) % ndp).wait_recv()
        all_targets = wanted[...].astype(f32).reshape(ndp * slots, seq)
        seen = jnp.dot(slot_hot[...], all_targets, precision=HIGH, preferred_element_type=f32)
        position = lax.broadcasted_iota(jnp.int32, (tokens, seq), 1)
        row = lax.broadcasted_iota(jnp.int32, (tokens, seq), 0)
        target_col[...] = jnp.sum(
            jnp.where(position == row % seq, seen, 0.0), axis=1, keepdims=True
        ).astype(jnp.int32)

    tree_gather(out_block, spread_send, spread_recv, {2: send_targets, 6: target_work})

    block = 256

    @pl.loop(0, 2 * vocab // block)
    def _(i):
        cols = pl.ds(pl.multiple_of(i * block, block), block)
        logits[:, cols] = jnp.dot(normed_out[...], out[:, cols], preferred_element_type=f32)

    ntile = 2 * vocab // 128

    @pl.loop(0, tokens // row_step)
    def _(i):
        rows = pl.ds(pl.multiple_of(i * row_step, row_step), row_step)

        def load(k):
            return logits[rows, k * 128 : (k + 1) * 128]

        top = load(0)
        for k in range(1, ntile):
            top = jnp.maximum(top, load(k))
        top = jnp.max(top, axis=1, keepdims=True)
        place = lax.broadcasted_iota(jnp.int32, (row_step, 128), 1)
        spot = target_col[rows, :] - z * (2 * vocab) - place
        total = jnp.zeros((row_step, 128), f32)
        hits = jnp.zeros((row_step, 128), f32)
        for k in range(ntile):
            tile = load(k)
            total = total + jnp.exp(tile - top)
            hits = hits + jnp.where(spot == k * 128, tile, 0.0)
        local = top + jnp.log(jnp.sum(total, axis=1, keepdims=True))
        picked = jnp.sum(hits, axis=1, keepdims=True)
        columns[rows, :] = jnp.where(place == 0, local, jnp.where(place == 1, picked, 0.0))

    turned = columns[...].T
    ngroup = tokens // 128
    for g in range(ngroup):
        stats[z, g : g + 1, :] = turned[0:1, g * 128 : (g + 1) * 128]
        stats[z, ngroup + g : ngroup + g + 1, :] = turned[1:2, g * 128 : (g + 1) * 128]

    for i in range(1, nz):
        send(remote(stats.at[z], stats.at[z], stat_send.at[i], stat_recv.at[i], z_peer(i)))
    for i in range(1, nz):
        place = stats.at[(z - i + nz) % nz]
        remote(place, place, stat_send.at[i], stat_recv.at[i], z_peer(i)).wait_recv()
    parts = [stats[i] for i in range(nz)]
    sums = [part[:ngroup] for part in parts]
    top = sums[0]
    for part in sums[1:]:
        top = jnp.maximum(top, part)
    total = add_up([jnp.exp(part - top) for part in sums])
    picked = add_up([part[ngroup:] for part in parts])
    lane_lp[...] = picked - (top + jnp.log(total))

    swap = remote(lane_lp, other_lp, pair_send, pair_recv, sibling)
    send(swap)
    swap.wait_recv()
    difference = jnp.where(
        core == 0, lane_lp[...] - other_lp[...], other_lp[...] - lane_lp[...]
    )
    diffs[dp] = difference

    for i in range(1, ndp):
        send(
            remote(
                diffs.at[dp], diffs.at[dp], diff_send.at[i], diff_recv.at[i], ((dp + i) % ndp, mp)
            )
        )
    for i in range(1, ndp):
        place = diffs.at[(dp - i + ndp) % ndp]
        remote(place, place, diff_send.at[i], diff_recv.at[i], ((dp + i) % ndp, mp)).wait_recv()

    per_group = slots // ngroup
    taken = []
    for g in range(ngroup):
        hot = select[g * per_group * slots : (g + 1) * per_group * slots, :]
        got = jnp.dot(hot, diffs[:, g, :], precision=HIGH, preferred_element_type=f32)
        row = lax.broadcasted_iota(jnp.int32, got.shape, 0) // slots
        lane = lax.broadcasted_iota(jnp.int32, got.shape, 1) // seq
        got = jnp.where(row == lane, got, 0.0)
        taken += [got[j * slots : (j + 1) * slots] for j in range(per_group)]
    fold = jnp.where(
        lax.broadcasted_iota(jnp.int32, (128, seq), 0) % seq
        == lax.broadcasted_iota(jnp.int32, (128, seq), 1),
        1.0,
        0.0,
    )
    moved = jnp.dot(add_up(taken), fold, precision=HIGH, preferred_element_type=f32)
    here = lax.broadcasted_iota(jnp.int32, (slots, slots), 0)
    there = lax.broadcasted_iota(jnp.int32, (slots, slots), 1)
    long = jnp.sum(jnp.where(here == there, lengths[...].astype(f32), 0.0), axis=1, keepdims=True)
    live = lax.broadcasted_iota(jnp.int32, (slots, seq), 1).astype(f32) < long
    kept = jnp.where(live, moved, 0.0)
    token_diff[...] = kept
    in_all = jnp.sum(kept, axis=1, keepdims=True)
    seq_diff[...] = jnp.sum(jnp.where(here == there, in_all, 0.0), axis=0, keepdims=True)

    for i in range(4):
        swap_done(i)
    for copy in waits:
        copy.wait_send()


def local(
    nz,
    hidden_policy,
    hidden_reference,
    ffn_gain_policy,
    ffn_gain_reference,
    up_policy,
    up_reference,
    down_policy,
    down_reference,
    final_gain_policy,
    final_gain_reference,
    out_policy,
    out_reference,
    move_plan,
    lengths,
    targets,
):
    slots, seq, part = hidden_policy.shape
    tokens = slots * seq
    width = up_policy.shape[0]
    units = up_policy.shape[1]
    vocab = out_policy.shape[1]
    ndp = SIDE * SIDE
    own = tokens // nz
    ngroup = tokens // 128
    plus = nz // 2
    any_space = pl.BlockSpec(memory_space=pl.ANY)
    vmem = pl.BlockSpec(memory_space=pltpu.VMEM)
    dma = pltpu.SemaphoreType.DMA
    ring = (2, plus, SUBS)
    token_diff, seq_diff = pl.pallas_call(
        functools.partial(kernel, nz),
        out_shape=(
            jax.ShapeDtypeStruct((slots, seq), f32),
            jax.ShapeDtypeStruct((1, slots), f32),
        ),
        in_specs=[any_space] * 15,
        out_specs=(vmem, vmem),
        scratch_shapes=[
            pltpu.VMEM((1, ndp * slots), jnp.int32),
            pltpu.VMEM((1, slots), jnp.int32),
            pltpu.VMEM((2, 1, width), f32),
            pltpu.VMEM((width // 128, own, 128), f32),
            pltpu.VMEM((2, tokens, part), bf16),
            pltpu.VMEM((width // 128, tokens, 128), bf16),
            pltpu.VMEM((tokens, width), bf16),
            pltpu.VMEM((width, 2 * units), bf16),
            pltpu.VMEM((2 * units, width), bf16),
            pltpu.VMEM((width, 2 * vocab), bf16),
            pltpu.VMEM((tokens, width), f32),
            pltpu.VMEM((2, plus, own, width), SUM_TYPE),
            pltpu.VMEM((2, plus, own, width), SUM_TYPE),
            pltpu.VMEM((tokens, width), bf16),
            pltpu.VMEM((tokens, 2 * vocab), f32),
            pltpu.VMEM((tokens, 128), f32),
            pltpu.VMEM((ndp, slots, seq), jnp.int32),
            pltpu.VMEM((tokens, 1), jnp.int32),
            pltpu.VMEM((tokens, ndp * slots), f32),
            pltpu.VMEM((slots * slots, ndp), f32),
            pltpu.VMEM((nz, 2 * ngroup, 128), f32),
            pltpu.VMEM((ngroup, 128), f32),
            pltpu.VMEM((ngroup, 128), f32),
            pltpu.VMEM((ndp, ngroup, 128), f32),
            dma((9,)),
            dma((4,)),
            dma((4,)),
            dma(ring),
            dma(ring),
            dma(ring),
            dma(ring),
            dma(ring),
            dma(ring),
            dma((2, 2, 2)),
            dma((2, 2, 2)),
            dma((2, 4, 2, 2)),
            dma((2, 4, 2, 2)),
            dma((ndp,)),
            dma((ndp,)),
            dma((nz,)),
            dma((nz,)),
            dma,
            dma,
            dma((ndp,)),
            dma((ndp,)),
        ],
        compiler_params=pltpu.CompilerParams(
            collective_id=0, has_side_effects=True, vmem_limit_bytes=60 * 1024 * 1024
        ),
        name="score",
    )(
        hidden_policy.reshape(tokens, part),
        hidden_reference.reshape(tokens, part),
        ffn_gain_policy.reshape(1, width),
        ffn_gain_reference.reshape(1, width),
        up_policy,
        up_reference,
        down_policy,
        down_reference,
        final_gain_policy.reshape(1, width),
        final_gain_reference.reshape(1, width),
        out_policy,
        out_reference,
        move_plan.reshape(1, ndp * slots),
        lengths.reshape(1, slots),
        targets,
    )
    return token_diff, seq_diff.reshape(slots)


def solution(mesh):
    nz = mesh.shape["mp"] // 2
    return jax.shard_map(
        functools.partial(local, nz),
        mesh=mesh,
        in_specs=(
            P("dp", None, "mp"),
            P("dp", None, "mp"),
            P(),
            P(),
            P(None, "mp"),
            P(None, "mp"),
            P("mp", None),
            P("mp", None),
            P(),
            P(),
            P("dp", "mp"),
            P("dp", "mp"),
            P(),
            P("dp"),
            P("dp", None),
        ),
        out_specs=(P("dp", None), P("dp")),
        check_vma=False,
    )
```

```python
import functools

import jax
import jax.numpy as jnp
from jax import lax
from jax.experimental import pallas as pl
from jax.experimental.pallas import tpu as pltpu
from jax.sharding import PartitionSpec as P

MESH = pl.DeviceIdType.MESH
EPS = 1e-05
SIDE = 4
SUBS = 2
SUM_TYPE = jnp.bfloat16
HIGH = lax.Precision.HIGHEST
f32 = jnp.float32
bf16 = jnp.bfloat16


def remote(src, dst, send_sem, recv_sem, device):
    return pltpu.make_async_remote_copy(
        src_ref=src,
        dst_ref=dst,
        send_sem=send_sem,
        recv_sem=recv_sem,
        device_id=device,
        device_id_type=MESH,
    )


def add_up(parts):
    while len(parts) > 1:
        parts = [
            parts[i] + parts[i + 1] if i + 1 < len(parts) else parts[i]
            for i in range(0, len(parts), 2)
        ]
    return parts[0]


def normed_tiles(load, count, gain, width, store):
    center = jnp.sum(add_up([load(i) for i in range(count)]), axis=1, keepdims=True) / width
    squares = [jnp.square(load(i) - center) for i in range(count)]
    spread = jnp.sum(add_up(squares), axis=1, keepdims=True) / width
    scale = lax.rsqrt(spread + EPS)
    for i in range(count):
        tile = (load(i) - center) * scale * gain[:, i * 128 : (i + 1) * 128]
        store(i, tile.astype(bf16))


def kernel(
    nz,
    hidden_p,
    hidden_r,
    ffn_gain_p,
    ffn_gain_r,
    up_p,
    up_r,
    down_p,
    down_r,
    final_gain_p,
    final_gain_r,
    out_p,
    out_r,
    plan_hbm,
    lengths_hbm,
    targets,
    token_diff,
    seq_diff,
    plan_row,
    lengths,
    gains,
    after,
    halves,
    feats,
    normed_in,
    up,
    down,
    out,
    partial,
    sums_out,
    sums_in,
    normed_out,
    logits,
    columns,
    wanted,
    target_col,
    slot_hot,
    select,
    stats,
    lps,
    local_sem,
    swap_send,
    swap_recv,
    gather_send,
    gather_recv,
    sum_send,
    sum_recv,
    spread_send,
    spread_recv,
    near_send,
    near_recv,
    far_send,
    far_recv,
    target_send,
    target_recv,
    stat_send,
    stat_recv,
    lp_send,
    lp_recv,
):
    dp = lax.axis_index("dp")
    mp = lax.axis_index("mp")
    z, core = mp // 2, mp % 2
    x, y = dp // SIDE, dp % SIDE
    ndp = SIDE * SIDE
    tokens, width = normed_out.shape
    slots, seq = token_diff.shape
    nfeat = width // 128
    own_tokens = tokens // nz
    units = up_p.shape[1]
    vocab = out_p.shape[1]
    depth = out_p.shape[0]
    piece = depth // 2
    quarter = piece // 2
    waits = []

    far_first_z = sorted(range(1, nz), key=lambda i: -min(i, nz - i))
    far_first_dp = sorted(
        range(1, ndp),
        key=lambda i: -min(i // SIDE, SIDE - i // SIDE) - min(i % SIDE, SIDE - i % SIDE),
    )

    def z_peer(step):
        return (dp, ((z + step + nz) % nz) * 2 + core)

    def xy_peer(axis, step):
        if axis == 0:
            return (((x + step + SIDE) % SIDE) * SIDE + y, mp)
        return (x * SIDE + (y + step + SIDE) % SIDE, mp)

    sibling = (dp, z * 2 + 1 - core)

    def send(copy):
        copy.start()
        waits.append(copy)

    def settle(copies):
        for copy in copies:
            copy.wait_send()
        copies.clear()

    own_rows = pl.ds(pl.multiple_of(dp * depth, depth), depth)

    def places(c):
        return (
            halves.at[c],
            out.at[own_rows, c * vocab : (c + 1) * vocab],
            up.at[:, c * units : (c + 1) * units],
            down.at[c * units : (c + 1) * units, :],
        )

    policy = (hidden_p, out_p, up_p, down_p, ffn_gain_p, final_gain_p)
    refer = (hidden_r, out_r, up_r, down_r, ffn_gain_r, final_gain_r)

    def local_copy(c, i):
        mine = policy if c == 0 else refer
        place = gains.at[i - 4] if i >= 4 else places(c)[i]
        return pltpu.make_async_copy(mine[i], place, local_sem.at[i])

    small_copies = [
        pltpu.make_async_copy(plan_hbm, plan_row, local_sem.at[6]),
        pltpu.make_async_copy(lengths_hbm, lengths, local_sem.at[7]),
        pltpu.make_async_copy(targets, wanted.at[dp], local_sem.at[8]),
    ]
    for c in (0, 1):

        @pl.when(core == c)
        def _(c=c):
            for i in range(6):
                local_copy(c, i).start()

    for copy in small_copies:
        copy.start()

    barrier = pltpu.get_barrier_semaphore()
    greeted = [sibling] + [z_peer(step) for step in (1, -1, 2, -2)]
    greeted += [xy_peer(axis, step) for axis in (0, 1) for step in (1, -1)]
    for device in greeted:
        pl.semaphore_signal(barrier, inc=1, device_id=device, device_id_type=MESH)
    pl.semaphore_wait(barrier, len(greeted))

    for c in (0, 1):

        @pl.when(core == c)
        def _(c=c):
            theirs = refer if c == 0 else policy
            remote(theirs[0], places(c)[0], swap_send.at[0], swap_recv.at[0], sibling).start()

    def swap_wait(i):
        for c in (0, 1):

            @pl.when(core == c)
            def _(c=c):
                theirs = refer if c == 0 else policy
                remote(
                    theirs[i], places(1 - c)[i], swap_send.at[i], swap_recv.at[i], sibling
                ).wait_recv()
                local_copy(c, i).wait()

    def swap_done(i):
        for c in (0, 1):

            @pl.when(core == c)
            def _(c=c):
                theirs = refer if c == 0 else policy
                remote(
                    theirs[i], places(c)[i], swap_send.at[i], swap_recv.at[i], sibling
                ).wait_send()

    plus, minus = nz // 2, nz // 2 - 1

    half = plus // 2
    ways = ((0, 1), (1, -1))

    def reach(way, sub):
        return plus if (sub < (SUBS + 1) // 2) == (way == 0) else minus

    def tree_gather(place, far_place, send_sem, recv_sem, hooks):
        def arrived(way, step, t, sub):
            block = place(step, t, sub)
            sems = send_sem.at[way, t - 1, sub], recv_sem.at[way, t - 1, sub]
            remote(block, block, *sems, z_peer(step)).wait_recv()

        def wait_odd(first, last):
            for t in range(first, last, 2):
                for sub in range(SUBS):
                    for way, step in ways:
                        if t <= reach(way, sub):
                            arrived(way, step, t, sub)

        for held in range(0, plus + 1, 2):
            for sub in range(SUBS):
                for way, step in ways:
                    hops = reach(way, sub)
                    if 0 < held <= hops:
                        arrived(way, step, held, sub)
                    for far in (2, 1):
                        t = held + far
                        if t <= hops:
                            sems = send_sem.at[way, t - 1, sub], recv_sem.at[way, t - 1, sub]
                            block = place(step, held, sub)
                            there = far_place(step, held, t, sub)
                            send(remote(block, there, *sems, z_peer(step * far)))
            if held == half:
                wait_odd(1, half)
            if held in hooks:
                hooks[held]()
        wait_odd(half + 1, plus + 1)

    def block_rows(h, along, across, part):
        first, second = (along, across) if h == 0 else (across, along)
        start = (first * SIDE + second) * depth + h * piece
        if part is None:
            return out.at[pl.ds(pl.multiple_of(start, piece), piece), :]
        return out.at[pl.ds(pl.multiple_of(start + part * quarter, quarter), quarter), :]

    def place_of(h):
        return (x, y) if h == 0 else (y, x)

    def along_of(h, j):
        return (place_of(h)[0] + (0, -1, 1, 2)[j] + SIDE) % SIDE

    def near(h, way, forward):
        step = (1, -1)[way]
        u, v = place_of(h)
        if forward:
            rows = block_rows(h, (u - step + SIDE) % SIDE, v, way)
        else:
            rows = block_rows(h, u, v, None)
        sem = (h, way, int(forward))
        return remote(rows, rows, near_send.at[sem], near_recv.at[sem], xy_peer(h, step))

    def near_wait(h, way, forward):
        step = (1, -1)[way]
        u, v = place_of(h)
        if forward:
            rows = block_rows(h, (u - 2 * step + SIDE) % SIDE, v, way)
        else:
            rows = block_rows(h, (u - step + SIDE) % SIDE, v, None)
        sem = (h, way, int(forward))
        remote(rows, rows, near_send.at[sem], near_recv.at[sem], xy_peer(h, step)).wait_recv()

    def far(h, j, way, forward):
        step = (1, -1)[way]
        v = place_of(h)[1]
        if forward:
            rows = block_rows(h, along_of(h, j), (v - step + SIDE) % SIDE, way)
        else:
            rows = block_rows(h, along_of(h, j), v, None)
        sem = (h, j, way, int(forward))
        return remote(rows, rows, far_send.at[sem], far_recv.at[sem], xy_peer(1 - h, step))

    def far_wait(h, j, way, forward):
        step = (1, -1)[way]
        v = place_of(h)[1]
        if forward:
            rows = block_rows(h, along_of(h, j), (v - 2 * step + SIDE) % SIDE, way)
        else:
            rows = block_rows(h, along_of(h, j), (v - step + SIDE) % SIDE, None)
        sem = (h, j, way, int(forward))
        remote(rows, rows, far_send.at[sem], far_recv.at[sem], xy_peer(1 - h, step)).wait_recv()

    both = [(h, way) for h in (0, 1) for way in (0, 1)]

    def out_round_0():
        swap_wait(1)
        for h, way in both:
            send(near(h, way, False))
        for h, way in both:
            send(far(h, 0, way, False))

    def out_round_1():
        for h, way in both:
            near_wait(h, way, False)
            send(near(h, way, True))
        for j in (1, 2):
            for h, way in both:
                send(far(h, j, way, False))
        for h, way in both:
            far_wait(h, 0, way, False)
            send(far(h, 0, way, True))

    def out_round_2():
        for h, way in both:
            near_wait(h, way, True)
        for h, way in both:
            send(far(h, 3, way, False))
        for j in (1, 2):
            for h, way in both:
                far_wait(h, j, way, False)
                send(far(h, j, way, True))

    def out_round_3():
        for h, way in both:
            far_wait(h, 3, way, False)
            send(far(h, 3, way, True))

    def out_round_4():
        for j in range(4):
            for h, way in both:
                far_wait(h, j, way, True)

    swap_wait(0)
    feats[z] = jnp.concatenate([halves[0], halves[1]], axis=1)
    sub_tokens = tokens // SUBS

    def feat_place(step, t, sub):
        source = (z - step * t + nz) % nz
        return feats.at[source, sub * sub_tokens : (sub + 1) * sub_tokens, :]

    def feat_far_place(step, held, t, sub):
        return feat_place(step, held, sub)

    def whole_order(row):
        block = (row // own_tokens + (z + nz - half)) % nz
        return block * own_tokens + row % own_tokens

    def index_work():
        for copy in small_copies:
            copy.wait()
        request = lax.broadcasted_iota(jnp.int32, (slots, ndp * slots), 1)
        order = lax.broadcasted_iota(jnp.int32, (slots, ndp * slots), 0)
        spread_plan = jnp.where(request % slots == order, plan_row[...], 0).astype(bf16)
        request = lax.broadcasted_iota(jnp.int32, (ndp * slots, ndp), 0)
        holder = lax.broadcasted_iota(jnp.int32, (ndp * slots, ndp), 1)
        owner = jnp.where(request // slots == holder, 1.0, 0.0).astype(bf16)
        plan = jnp.dot(spread_plan, owner, preferred_element_type=f32)
        slot_id = lax.broadcasted_iota(jnp.int32, (slots, slots, ndp), 1) + dp * slots
        hot = jnp.broadcast_to(plan[:, None, :], (slots, slots, ndp)) == slot_id.astype(f32)
        select[...] = jnp.where(hot, 1.0, 0.0).reshape(slots * slots, ndp)
        token = lax.broadcasted_iota(jnp.int32, (tokens, ndp * slots), 0)
        lane = lax.broadcasted_iota(jnp.int32, (tokens, ndp * slots), 1)
        own_request = lane == dp * slots + whole_order(token) // seq
        owner_slot = jnp.sum(
            jnp.where(own_request, plan_row[...].astype(f32), 0.0), axis=1, keepdims=True
        )
        slot_hot[...] = jnp.where(lane.astype(f32) == owner_slot, 1.0, 0.0)

    def first_hook():
        for c in (0, 1):

            @pl.when(core == c)
            def _(c=c):
                theirs = refer if c == 0 else policy
                for i, place in enumerate(places(c)):
                    if i:
                        remote(theirs[i], place, swap_send.at[i], swap_recv.at[i], sibling).start()

        out_round_0()
        index_work()

    hooks = {0: first_hook, half: out_round_1}
    tree_gather(feat_place, feat_far_place, gather_send, gather_recv, hooks)

    for i in (4, 5):
        for c in (0, 1):

            @pl.when(core == c)
            def _(c=c, i=i):
                local_copy(c, i).wait()

    row_step = min(64, tokens)

    @pl.loop(0, tokens // row_step)
    def _(i):
        rows = pl.ds(pl.multiple_of(i * row_step, row_step), row_step)

        def store(k, tile):
            normed_in[rows, k * 128 : (k + 1) * 128] = tile

        normed_tiles(lambda k: feats[k, rows, :].astype(f32), nfeat, gains[0], width, store)

    swap_wait(2)
    swap_wait(3)
    pre = jnp.dot(normed_in[...], up[...], preferred_element_type=f32)
    active = jax.nn.gelu(pre).astype(bf16)

    sub_width = width // SUBS

    def rows_of(chunk):
        return pl.ds(pl.multiple_of(chunk * own_tokens, own_tokens), own_tokens)

    def sum_copy(way, t, sub):
        cols = slice(sub * sub_width, (sub + 1) * sub_width)
        return remote(
            sums_out.at[way, t - 1, :, cols],
            sums_in.at[way, t - 1, :, cols],
            sum_send.at[way, t - 1, sub],
            sum_recv.at[way, t - 1, sub],
            z_peer((1, -1)[way] * (1 if t % 2 else 2)),
        )

    def hand_on(t):
        for sub in range(SUBS):
            cols = slice(sub * sub_width, (sub + 1) * sub_width)
            if t == plus:
                partial[:, cols] = jnp.dot(active, down[:, cols], preferred_element_type=f32)
            for way, step in ways:
                hops = reach(way, sub)
                if t > hops:
                    continue
                term = partial[rows_of((z + step * t + nz) % nz), cols]
                if t % 2 == 0:
                    for behind in (t + 2, t + 1):
                        if behind <= hops:
                            sum_copy(way, behind, sub).wait_recv()
                            term = term + sums_in[way, behind - 1, :, cols].astype(f32)
                sums_out[way, t - 1, :, cols] = term.astype(sums_out.dtype)
                send(sum_copy(way, t, sub))

    hand_on(plus)
    hand_on(plus - 1)
    for t in range(plus - 2, 0, -2):
        hand_on(t - 1)
        hand_on(t)
        if t == plus - 2:
            out_round_2()
    out_round_3()
    for t in (1, 2):
        for sub in range(SUBS):
            for way in (0, 1):
                sum_copy(way, t, sub).wait_recv()

    mine = rows_of(z)
    for k in range(nfeat):
        cols = slice(k * 128, (k + 1) * 128)
        came = [sums_in[way, t, :, cols].astype(f32) for way in (0, 1) for t in (0, 1)]
        total = partial[mine, cols] + add_up(came)
        after[k] = feats[k, mine, :].astype(f32) + total

    def store_out(k, tile):
        normed_out[half * own_tokens : (half + 1) * own_tokens, k * 128 : (k + 1) * 128] = tile

    normed_tiles(lambda k: after[k], nfeat, gains[1], width, store_out)

    def out_place(step, t, sub):
        slot = (half - step * t + nz) % nz
        cols = slice(sub * sub_width, (sub + 1) * sub_width)
        return normed_out.at[slot * own_tokens : (slot + 1) * own_tokens, cols]

    def out_far_place(step, held, t, sub):
        return out_place(step, t, sub)

    def target_copy(i, source):
        return remote(
            wanted.at[source],
            wanted.at[source],
            target_send,
            target_recv,
            ((dp + i) % ndp, mp),
        )

    def send_targets():
        out_round_4()
        for i in range(1, ndp):
            target_copy(i, dp).start()

    def settle_early():
        for i in range(4):
            swap_done(i)
        settle(early)

    def target_work():
        others = wanted.at[0 : ndp - 1]
        every = remote(others, others, target_send, target_recv, sibling)
        every.wait_send()
        every.wait_recv()
        all_targets = wanted[...].astype(f32).reshape(ndp * slots, seq)
        seen = jnp.dot(slot_hot[...], all_targets, precision=HIGH, preferred_element_type=f32)
        position = lax.broadcasted_iota(jnp.int32, (tokens, seq), 1)
        row = lax.broadcasted_iota(jnp.int32, (tokens, seq), 0)
        target_col[...] = jnp.sum(
            jnp.where(position == whole_order(row) % seq, seen, 0.0), axis=1, keepdims=True
        ).astype(jnp.int32)

    block = 256
    ntile = 2 * vocab // 128

    def score(first, last):
        rows = slice(first * own_tokens, last * own_tokens)

        @pl.loop(0, 2 * vocab // block)
        def _(i):
            cols = pl.ds(pl.multiple_of(i * block, block), block)
            logits[rows, cols] = jnp.dot(
                normed_out[rows, :], out[:, cols], preferred_element_type=f32
            )

    def summarize(first, last):
        rows = slice(first * own_tokens, last * own_tokens)
        shape = ((last - first) * own_tokens, 128)

        def load(k):
            return logits[rows, k * 128 : (k + 1) * 128]

        top = load(0)
        for k in range(1, ntile):
            top = jnp.maximum(top, load(k))
        top = jnp.max(top, axis=1, keepdims=True)
        place = lax.broadcasted_iota(jnp.int32, shape, 1)
        spot = target_col[rows, :] - z * (2 * vocab) - place
        total = jnp.zeros(shape, f32)
        hits = jnp.zeros(shape, f32)
        for k in range(ntile):
            tile = load(k)
            total = total + jnp.exp(tile - top)
            hits = hits + jnp.where(spot == k * 128, tile, 0.0)
        local = top + jnp.log(jnp.sum(total, axis=1, keepdims=True))
        picked = jnp.sum(hits, axis=1, keepdims=True)
        values = jnp.where(place == 0, local, jnp.where(place == 1, picked, 0.0))
        for i in range(first, last):
            block_rows = values[(i - first) * own_tokens : (i - first + 1) * own_tokens]
            columns[rows_of((z + i + nz - half) % nz), :] = block_rows

    def summarize_all(first, last):
        for i in range(first, last, 3):
            summarize(i, min(i + 3, last))

    near_blocks = 2 * half + 1

    def before_far():
        target_work()
        summarize_all(0, near_blocks)

    def after_relay():
        send_targets()
        settle_early()

    early = list(waits)
    waits.clear()
    hooks = {2: after_relay, half: lambda: score(0, near_blocks), plus - 2: before_far}
    tree_gather(out_place, out_far_place, spread_send, spread_recv, hooks)
    score(near_blocks, nz)
    summarize_all(near_blocks, nz)

    turned = columns[...].T
    ngroup = tokens // 128
    for g in range(ngroup):
        stats[z, g : g + 1, :] = turned[0:1, g * 128 : (g + 1) * 128]
        stats[z, ngroup + g : ngroup + g + 1, :] = turned[1:2, g * 128 : (g + 1) * 128]

    for i in far_first_z:
        remote(stats.at[z], stats.at[z], stat_send, stat_recv, z_peer(i)).start()
    settle(waits)
    others = stats.at[0 : nz - 1]
    every = remote(others, others, stat_send, stat_recv, z_peer(1))
    every.wait_send()
    every.wait_recv()
    parts = [stats[i] for i in range(nz)]
    sums = [part[:ngroup] for part in parts]
    top = sums[0]
    for part in sums[1:]:
        top = jnp.maximum(top, part)
    total = add_up([jnp.exp(part - top) for part in sums])
    picked = add_up([part[ngroup:] for part in parts])
    lps[core * ndp + dp] = picked - (top + jnp.log(total))

    place = lps.at[core * ndp + dp]
    for step in far_first_dp + [0]:
        for turn in (0, 1):
            if step or turn:
                peer = ((x + step // SIDE) % SIDE) * SIDE + (y + step % SIDE) % SIDE
                device = (peer, z * 2 + (core + turn) % 2)
                remote(place, place, lp_send, lp_recv, device).start()
    others = lps.at[0 : 2 * ndp - 1]
    every = remote(others, others, lp_send, lp_recv, sibling)
    every.wait_recv()

    per_group = slots // ngroup
    taken = []
    for g in range(ngroup):
        hot = select[g * per_group * slots : (g + 1) * per_group * slots, :]
        between = lps[:ndp, g, :] - lps[ndp:, g, :]
        got = jnp.dot(hot, between, precision=HIGH, preferred_element_type=f32)
        row = lax.broadcasted_iota(jnp.int32, got.shape, 0) // slots
        lane = lax.broadcasted_iota(jnp.int32, got.shape, 1) // seq
        got = jnp.where(row == lane, got, 0.0)
        taken += [got[j * slots : (j + 1) * slots] for j in range(per_group)]
    fold = jnp.where(
        lax.broadcasted_iota(jnp.int32, (128, seq), 0) % seq
        == lax.broadcasted_iota(jnp.int32, (128, seq), 1),
        1.0,
        0.0,
    )
    moved = jnp.dot(add_up(taken), fold, precision=HIGH, preferred_element_type=f32)
    here = lax.broadcasted_iota(jnp.int32, (slots, slots), 0)
    there = lax.broadcasted_iota(jnp.int32, (slots, slots), 1)
    long = jnp.sum(jnp.where(here == there, lengths[...].astype(f32), 0.0), axis=1, keepdims=True)
    live = lax.broadcasted_iota(jnp.int32, (slots, seq), 1).astype(f32) < long
    kept = jnp.where(live, moved, 0.0)
    token_diff[...] = kept
    in_all = jnp.sum(kept, axis=1, keepdims=True)
    seq_diff[...] = jnp.sum(jnp.where(here == there, in_all, 0.0), axis=0, keepdims=True)

    every.wait_send()


def local(
    nz,
    hidden_policy,
    hidden_reference,
    ffn_gain_policy,
    ffn_gain_reference,
    up_policy,
    up_reference,
    down_policy,
    down_reference,
    final_gain_policy,
    final_gain_reference,
    out_policy,
    out_reference,
    move_plan,
    lengths,
    targets,
):
    slots, seq, part = hidden_policy.shape
    tokens = slots * seq
    width = up_policy.shape[0]
    units = up_policy.shape[1]
    vocab = out_policy.shape[1]
    ndp = SIDE * SIDE
    own = tokens // nz
    ngroup = tokens // 128
    plus = nz // 2
    any_space = pl.BlockSpec(memory_space=pl.ANY)
    vmem = pl.BlockSpec(memory_space=pltpu.VMEM)
    dma = pltpu.SemaphoreType.DMA
    ring = (2, plus, SUBS)
    token_diff, seq_diff = pl.pallas_call(
        functools.partial(kernel, nz),
        out_shape=(
            jax.ShapeDtypeStruct((slots, seq), f32),
            jax.ShapeDtypeStruct((1, slots), f32),
        ),
        in_specs=[any_space] * 15,
        out_specs=(vmem, vmem),
        scratch_shapes=[
            pltpu.VMEM((1, ndp * slots), jnp.int32),
            pltpu.VMEM((1, slots), jnp.int32),
            pltpu.VMEM((2, 1, width), f32),
            pltpu.VMEM((width // 128, own, 128), f32),
            pltpu.VMEM((2, tokens, part), bf16),
            pltpu.VMEM((width // 128, tokens, 128), bf16),
            pltpu.VMEM((tokens, width), bf16),
            pltpu.VMEM((width, 2 * units), bf16),
            pltpu.VMEM((2 * units, width), bf16),
            pltpu.VMEM((width, 2 * vocab), bf16),
            pltpu.VMEM((tokens, width), f32),
            pltpu.VMEM((2, plus, own, width), SUM_TYPE),
            pltpu.VMEM((2, plus, own, width), SUM_TYPE),
            pltpu.VMEM((tokens, width), bf16),
            pltpu.VMEM((tokens, 2 * vocab), f32),
            pltpu.VMEM((tokens, 128), f32),
            pltpu.VMEM((ndp, slots, seq), jnp.int32),
            pltpu.VMEM((tokens, 1), jnp.int32),
            pltpu.VMEM((tokens, ndp * slots), f32),
            pltpu.VMEM((slots * slots, ndp), f32),
            pltpu.VMEM((nz, 2 * ngroup, 128), f32),
            pltpu.VMEM((2 * ndp, ngroup, 128), f32),
            dma((9,)),
            dma((4,)),
            dma((4,)),
            dma(ring),
            dma(ring),
            dma(ring),
            dma(ring),
            dma(ring),
            dma(ring),
            dma((2, 2, 2)),
            dma((2, 2, 2)),
            dma((2, 4, 2, 2)),
            dma((2, 4, 2, 2)),
            dma,
            dma,
            dma,
            dma,
            dma,
            dma,
        ],
        compiler_params=pltpu.CompilerParams(
            collective_id=0, has_side_effects=True, vmem_limit_bytes=60 * 1024 * 1024
        ),
        name="score",
    )(
        hidden_policy.reshape(tokens, part),
        hidden_reference.reshape(tokens, part),
        ffn_gain_policy.reshape(1, width),
        ffn_gain_reference.reshape(1, width),
        up_policy,
        up_reference,
        down_policy,
        down_reference,
        final_gain_policy.reshape(1, width),
        final_gain_reference.reshape(1, width),
        out_policy,
        out_reference,
        move_plan.reshape(1, ndp * slots),
        lengths.reshape(1, slots),
        targets,
    )
    def hand_over(token_in, seq_in, token_out, seq_out):
        token_out[...] = token_in[...]
        seq_out[...] = seq_in[...]

    token_diff, seq_diff = pl.pallas_call(
        hand_over,
        out_shape=(
            jax.ShapeDtypeStruct((slots, seq), f32),
            jax.ShapeDtypeStruct((1, slots), f32),
        ),
        name="hand_over",
    )(token_diff, seq_diff)
    return token_diff, seq_diff.reshape(slots)


def solution(mesh):
    nz = mesh.shape["mp"] // 2
    return jax.shard_map(
        functools.partial(local, nz),
        mesh=mesh,
        in_specs=(
            P("dp", None, "mp"),
            P("dp", None, "mp"),
            P(),
            P(),
            P(None, "mp"),
            P(None, "mp"),
            P("mp", None),
            P("mp", None),
            P(),
            P(),
            P("dp", "mp"),
            P("dp", "mp"),
            P(),
            P("dp"),
            P("dp", None),
        ),
        out_specs=(P("dp", None), P("dp")),
        check_vma=False,
    )
```

```python
import functools

import jax
import jax.numpy as jnp
from jax import lax
from jax.experimental import pallas as pl
from jax.experimental.pallas import tpu as pltpu
from jax.sharding import PartitionSpec as P

MESH = pl.DeviceIdType.MESH
EPS = 1e-05
SIDE = 4
SUBS = 2
SUM_TYPE = jnp.bfloat16
HIGH = lax.Precision.HIGHEST
f32 = jnp.float32
bf16 = jnp.bfloat16


def remote(src, dst, send_sem, recv_sem, device):
    return pltpu.make_async_remote_copy(
        src_ref=src,
        dst_ref=dst,
        send_sem=send_sem,
        recv_sem=recv_sem,
        device_id=device,
        device_id_type=MESH,
    )


def add_up(parts):
    while len(parts) > 1:
        parts = [
            parts[i] + parts[i + 1] if i + 1 < len(parts) else parts[i]
            for i in range(0, len(parts), 2)
        ]
    return parts[0]


def normed_tiles(load, count, gain, width, store):
    center = jnp.sum(add_up([load(i) for i in range(count)]), axis=1, keepdims=True) / width
    squares = [jnp.square(load(i) - center) for i in range(count)]
    spread = jnp.sum(add_up(squares), axis=1, keepdims=True) / width
    scale = lax.rsqrt(spread + EPS)
    for i in range(count):
        tile = (load(i) - center) * scale * gain[:, i * 128 : (i + 1) * 128]
        store(i, tile.astype(bf16))


def kernel(
    nz,
    hidden_p,
    hidden_r,
    ffn_gain_p,
    ffn_gain_r,
    up_p,
    up_r,
    down_p,
    down_r,
    final_gain_p,
    final_gain_r,
    out_p,
    out_r,
    plan_hbm,
    lengths_hbm,
    targets,
    token_diff,
    seq_diff,
    plan_row,
    lengths,
    gains,
    after,
    halves,
    feats,
    normed_in,
    up,
    down,
    out,
    partial,
    sums_out,
    sums_in,
    normed_out,
    logits,
    columns,
    wanted,
    target_col,
    slot_hot,
    select,
    stats,
    lps,
    local_sem,
    swap_send,
    swap_recv,
    gather_send,
    gather_recv,
    sum_send,
    sum_recv,
    spread_send,
    spread_recv,
    near_send,
    near_recv,
    far_send,
    far_recv,
    target_send,
    target_recv,
    stat_send,
    stat_recv,
    lp_send,
    lp_recv,
):
    dp = lax.axis_index("dp")
    mp = lax.axis_index("mp")
    z, core = mp // 2, mp % 2
    x, y = dp // SIDE, dp % SIDE
    ndp = SIDE * SIDE
    tokens, width = normed_out.shape
    slots, seq = token_diff.shape
    nfeat = width // 128
    own_tokens = tokens // nz
    units = up_p.shape[1]
    vocab = out_p.shape[1]
    depth = out_p.shape[0]
    piece = depth // 2
    quarter = piece // 2
    waits = []

    far_first_z = sorted(range(1, nz), key=lambda i: -min(i, nz - i))
    far_first_dp = sorted(
        range(1, ndp),
        key=lambda i: -min(i // SIDE, SIDE - i // SIDE) - min(i % SIDE, SIDE - i % SIDE),
    )

    def z_peer(step):
        return (dp, ((z + step + nz) % nz) * 2 + core)

    def xy_peer(axis, step):
        if axis == 0:
            return (((x + step + SIDE) % SIDE) * SIDE + y, mp)
        return (x * SIDE + (y + step + SIDE) % SIDE, mp)

    sibling = (dp, z * 2 + 1 - core)

    def send(copy):
        copy.start()
        waits.append(copy)

    def settle(copies):
        for copy in copies:
            copy.wait_send()
        copies.clear()

    own_rows = pl.ds(pl.multiple_of(dp * depth, depth), depth)

    def places(c):
        return (
            halves.at[c],
            out.at[own_rows, c * vocab : (c + 1) * vocab],
            up.at[:, c * units : (c + 1) * units],
            down.at[c * units : (c + 1) * units, :],
        )

    policy = (hidden_p, out_p, up_p, down_p, ffn_gain_p, final_gain_p)
    refer = (hidden_r, out_r, up_r, down_r, ffn_gain_r, final_gain_r)

    def local_copy(c, i):
        mine = policy if c == 0 else refer
        place = gains.at[i - 4] if i >= 4 else places(c)[i]
        return pltpu.make_async_copy(mine[i], place, local_sem.at[i])

    small_copies = [
        pltpu.make_async_copy(plan_hbm, plan_row, local_sem.at[6]),
        pltpu.make_async_copy(lengths_hbm, lengths, local_sem.at[7]),
        pltpu.make_async_copy(targets, wanted.at[dp], local_sem.at[8]),
    ]
    for c in (0, 1):

        @pl.when(core == c)
        def _(c=c):
            for i in range(6):
                local_copy(c, i).start()

    for copy in small_copies:
        copy.start()

    barrier = pltpu.get_barrier_semaphore()
    greeted = [sibling] + [z_peer(step) for step in (1, -1, 2, -2)]
    greeted += [xy_peer(axis, step) for axis in (0, 1) for step in (1, -1)]
    for device in greeted:
        pl.semaphore_signal(barrier, inc=1, device_id=device, device_id_type=MESH)
    pl.semaphore_wait(barrier, len(greeted))

    for c in (0, 1):

        @pl.when(core == c)
        def _(c=c):
            theirs = refer if c == 0 else policy
            remote(theirs[0], places(c)[0], swap_send.at[0], swap_recv.at[0], sibling).start()

    def swap_wait(i):
        for c in (0, 1):

            @pl.when(core == c)
            def _(c=c):
                theirs = refer if c == 0 else policy
                remote(
                    theirs[i], places(1 - c)[i], swap_send.at[i], swap_recv.at[i], sibling
                ).wait_recv()
                local_copy(c, i).wait()

    def swap_done(i):
        for c in (0, 1):

            @pl.when(core == c)
            def _(c=c):
                theirs = refer if c == 0 else policy
                remote(
                    theirs[i], places(c)[i], swap_send.at[i], swap_recv.at[i], sibling
                ).wait_send()

    plus, minus = nz // 2, nz // 2 - 1

    half = plus // 2
    ways = ((0, 1), (1, -1))

    def reach(way, sub):
        return plus if (sub < (SUBS + 1) // 2) == (way == 0) else minus

    def tree_gather(place, far_place, send_sem, recv_sem, hooks):
        def arrived(way, step, t, sub):
            block = place(step, t, sub)
            sems = send_sem.at[way, t - 1, sub], recv_sem.at[way, t - 1, sub]
            remote(block, block, *sems, z_peer(step)).wait_recv()

        def wait_odd(first, last):
            for t in range(first, last, 2):
                for sub in range(SUBS):
                    for way, step in ways:
                        if t <= reach(way, sub):
                            arrived(way, step, t, sub)

        for held in range(0, plus + 1, 2):
            late = []
            for sub in range(SUBS):
                for way, step in ways:
                    hops = reach(way, sub)
                    if 0 < held <= hops:
                        arrived(way, step, held, sub)
                    for far in (2, 1):
                        t = held + far
                        if t <= hops:
                            sems = send_sem.at[way, t - 1, sub], recv_sem.at[way, t - 1, sub]
                            block = place(step, held, sub)
                            there = far_place(step, held, t, sub)
                            copy = remote(block, there, *sems, z_peer(step * far))
                            if far == 1:
                                late.append(copy)
                            else:
                                send(copy)
            for copy in late:
                send(copy)
            if held == half:
                wait_odd(1, half)
            if held in hooks:
                hooks[held]()
        wait_odd(half + 1, plus + 1)

    def block_rows(h, along, across, part):
        first, second = (along, across) if h == 0 else (across, along)
        start = (first * SIDE + second) * depth + h * piece
        if part is None:
            return out.at[pl.ds(pl.multiple_of(start, piece), piece), :]
        return out.at[pl.ds(pl.multiple_of(start + part * quarter, quarter), quarter), :]

    def place_of(h):
        return (x, y) if h == 0 else (y, x)

    def along_of(h, j):
        return (place_of(h)[0] + (0, -1, 1, 2)[j] + SIDE) % SIDE

    def near(h, way, forward):
        step = (1, -1)[way]
        u, v = place_of(h)
        if forward:
            rows = block_rows(h, (u - step + SIDE) % SIDE, v, way)
        else:
            rows = block_rows(h, u, v, None)
        sem = (h, way, int(forward))
        return remote(rows, rows, near_send.at[sem], near_recv.at[sem], xy_peer(h, step))

    def near_wait(h, way, forward):
        step = (1, -1)[way]
        u, v = place_of(h)
        if forward:
            rows = block_rows(h, (u - 2 * step + SIDE) % SIDE, v, way)
        else:
            rows = block_rows(h, (u - step + SIDE) % SIDE, v, None)
        sem = (h, way, int(forward))
        remote(rows, rows, near_send.at[sem], near_recv.at[sem], xy_peer(h, step)).wait_recv()

    def far(h, j, way, forward):
        step = (1, -1)[way]
        v = place_of(h)[1]
        if forward:
            rows = block_rows(h, along_of(h, j), (v - step + SIDE) % SIDE, way)
        else:
            rows = block_rows(h, along_of(h, j), v, None)
        sem = (h, j, way, int(forward))
        return remote(rows, rows, far_send.at[sem], far_recv.at[sem], xy_peer(1 - h, step))

    def far_wait(h, j, way, forward):
        step = (1, -1)[way]
        v = place_of(h)[1]
        if forward:
            rows = block_rows(h, along_of(h, j), (v - 2 * step + SIDE) % SIDE, way)
        else:
            rows = block_rows(h, along_of(h, j), (v - step + SIDE) % SIDE, None)
        sem = (h, j, way, int(forward))
        remote(rows, rows, far_send.at[sem], far_recv.at[sem], xy_peer(1 - h, step)).wait_recv()

    both = [(h, way) for h in (0, 1) for way in (0, 1)]

    def out_round_0():
        swap_wait(1)
        for h, way in both:
            send(near(h, way, False))
        for h, way in both:
            send(far(h, 0, way, False))

    def out_round_1():
        for h, way in both:
            near_wait(h, way, False)
            send(near(h, way, True))
        for j in (1, 2):
            for h, way in both:
                send(far(h, j, way, False))
        for h, way in both:
            far_wait(h, 0, way, False)
            send(far(h, 0, way, True))

    def out_round_2():
        for h, way in both:
            near_wait(h, way, True)
        for h, way in both:
            send(far(h, 3, way, False))
        for j in (1, 2):
            for h, way in both:
                far_wait(h, j, way, False)
                send(far(h, j, way, True))

    def out_round_3():
        for h, way in both:
            far_wait(h, 3, way, False)
            send(far(h, 3, way, True))

    def out_round_4():
        for j in range(4):
            for h, way in both:
                far_wait(h, j, way, True)

    swap_wait(0)
    feats[z] = jnp.concatenate([halves[0], halves[1]], axis=1)
    sub_tokens = tokens // SUBS

    def feat_place(step, t, sub):
        source = (z - step * t + nz) % nz
        return feats.at[source, sub * sub_tokens : (sub + 1) * sub_tokens, :]

    def feat_far_place(step, held, t, sub):
        return feat_place(step, held, sub)

    def whole_order(row):
        block = (row // own_tokens + (z + nz - half)) % nz
        return block * own_tokens + row % own_tokens

    def index_work():
        for copy in small_copies:
            copy.wait()
        request = lax.broadcasted_iota(jnp.int32, (slots, ndp * slots), 1)
        order = lax.broadcasted_iota(jnp.int32, (slots, ndp * slots), 0)
        spread_plan = jnp.where(request % slots == order, plan_row[...], 0).astype(bf16)
        request = lax.broadcasted_iota(jnp.int32, (ndp * slots, ndp), 0)
        holder = lax.broadcasted_iota(jnp.int32, (ndp * slots, ndp), 1)
        owner = jnp.where(request // slots == holder, 1.0, 0.0).astype(bf16)
        plan = jnp.dot(spread_plan, owner, preferred_element_type=f32)
        slot_id = lax.broadcasted_iota(jnp.int32, (slots, slots, ndp), 1) + dp * slots
        hot = jnp.broadcast_to(plan[:, None, :], (slots, slots, ndp)) == slot_id.astype(f32)
        select[...] = jnp.where(hot, 1.0, 0.0).reshape(slots * slots, ndp)
        token = lax.broadcasted_iota(jnp.int32, (tokens, ndp * slots), 0)
        lane = lax.broadcasted_iota(jnp.int32, (tokens, ndp * slots), 1)
        own_request = lane == dp * slots + whole_order(token) // seq
        owner_slot = jnp.sum(
            jnp.where(own_request, plan_row[...].astype(f32), 0.0), axis=1, keepdims=True
        )
        slot_hot[...] = jnp.where(lane.astype(f32) == owner_slot, 1.0, 0.0)

    def first_hook():
        for c in (0, 1):

            @pl.when(core == c)
            def _(c=c):
                theirs = refer if c == 0 else policy
                for i, place in enumerate(places(c)):
                    if i:
                        remote(theirs[i], place, swap_send.at[i], swap_recv.at[i], sibling).start()

        out_round_0()
        index_work()

    hooks = {0: first_hook, half: out_round_1}
    tree_gather(feat_place, feat_far_place, gather_send, gather_recv, hooks)

    for i in (4, 5):
        for c in (0, 1):

            @pl.when(core == c)
            def _(c=c, i=i):
                local_copy(c, i).wait()

    row_step = min(64, tokens)

    @pl.loop(0, tokens // row_step)
    def _(i):
        rows = pl.ds(pl.multiple_of(i * row_step, row_step), row_step)

        def store(k, tile):
            normed_in[rows, k * 128 : (k + 1) * 128] = tile

        normed_tiles(lambda k: feats[k, rows, :].astype(f32), nfeat, gains[0], width, store)

    swap_wait(2)
    swap_wait(3)
    pre = jnp.dot(normed_in[...], up[...], preferred_element_type=f32)
    active = jax.nn.gelu(pre).astype(bf16)

    sub_width = width // SUBS

    def rows_of(chunk):
        return pl.ds(pl.multiple_of(chunk * own_tokens, own_tokens), own_tokens)

    def sum_copy(way, t, sub):
        cols = slice(sub * sub_width, (sub + 1) * sub_width)
        return remote(
            sums_out.at[way, t - 1, :, cols],
            sums_in.at[way, t - 1, :, cols],
            sum_send.at[way, t - 1, sub],
            sum_recv.at[way, t - 1, sub],
            z_peer((1, -1)[way] * (1 if t % 2 else 2)),
        )

    def hand_on(t):
        for sub in range(SUBS):
            cols = slice(sub * sub_width, (sub + 1) * sub_width)
            if t == plus:
                partial[:, cols] = jnp.dot(active, down[:, cols], preferred_element_type=f32)
            for way, step in ways:
                hops = reach(way, sub)
                if t > hops:
                    continue
                term = partial[rows_of((z + step * t + nz) % nz), cols]
                if t % 2 == 0:
                    for behind in (t + 2, t + 1):
                        if behind <= hops:
                            sum_copy(way, behind, sub).wait_recv()
                            term = term + sums_in[way, behind - 1, :, cols].astype(f32)
                sums_out[way, t - 1, :, cols] = term.astype(sums_out.dtype)
                send(sum_copy(way, t, sub))

    for t in range(plus, 0, -2):
        hand_on(t)
        if t == plus:
            hand_on(t - 1)
            hand_on(t - 3)
        elif t > 4:
            hand_on(t - 3)
        elif t == 4:
            hand_on(1)
        if t == plus - 2:
            out_round_2()
    out_round_3()
    for t in (1, 2):
        for sub in range(SUBS):
            for way in (0, 1):
                sum_copy(way, t, sub).wait_recv()

    mine = rows_of(z)
    for k in range(nfeat):
        cols = slice(k * 128, (k + 1) * 128)
        came = [sums_in[way, t, :, cols].astype(f32) for way in (0, 1) for t in (0, 1)]
        total = partial[mine, cols] + add_up(came)
        after[k] = feats[k, mine, :].astype(f32) + total

    def store_out(k, tile):
        normed_out[half * own_tokens : (half + 1) * own_tokens, k * 128 : (k + 1) * 128] = tile

    normed_tiles(lambda k: after[k], nfeat, gains[1], width, store_out)

    def out_place(step, t, sub):
        slot = (half - step * t + nz) % nz
        cols = slice(sub * sub_width, (sub + 1) * sub_width)
        return normed_out.at[slot * own_tokens : (slot + 1) * own_tokens, cols]

    def out_far_place(step, held, t, sub):
        return out_place(step, t, sub)

    def target_copy(i, source):
        return remote(
            wanted.at[source],
            wanted.at[source],
            target_send,
            target_recv,
            ((dp + i) % ndp, mp),
        )

    def send_targets():
        out_round_4()
        for i in range(1, ndp):
            target_copy(i, dp).start()

    def settle_early():
        for i in range(4):
            swap_done(i)
        settle(early)

    def target_work():
        others = wanted.at[0 : ndp - 1]
        every = remote(others, others, target_send, target_recv, sibling)
        every.wait_send()
        every.wait_recv()
        all_targets = wanted[...].astype(f32).reshape(ndp * slots, seq)
        seen = jnp.dot(slot_hot[...], all_targets, precision=HIGH, preferred_element_type=f32)
        position = lax.broadcasted_iota(jnp.int32, (tokens, seq), 1)
        row = lax.broadcasted_iota(jnp.int32, (tokens, seq), 0)
        target_col[...] = jnp.sum(
            jnp.where(position == whole_order(row) % seq, seen, 0.0), axis=1, keepdims=True
        ).astype(jnp.int32)

    block = 256
    ntile = 2 * vocab // 128

    def score(first, last):
        rows = slice(first * own_tokens, last * own_tokens)

        @pl.loop(0, 2 * vocab // block)
        def _(i):
            cols = pl.ds(pl.multiple_of(i * block, block), block)
            logits[rows, cols] = jnp.dot(
                normed_out[rows, :], out[:, cols], preferred_element_type=f32
            )

    def summarize(first, last):
        rows = slice(first * own_tokens, last * own_tokens)
        shape = ((last - first) * own_tokens, 128)

        def load(k):
            return logits[rows, k * 128 : (k + 1) * 128]

        top = load(0)
        for k in range(1, ntile):
            top = jnp.maximum(top, load(k))
        top = jnp.max(top, axis=1, keepdims=True)
        place = lax.broadcasted_iota(jnp.int32, shape, 1)
        spot = target_col[rows, :] - z * (2 * vocab) - place
        total = jnp.zeros(shape, f32)
        hits = jnp.zeros(shape, f32)
        for k in range(ntile):
            tile = load(k)
            total = total + jnp.exp(tile - top)
            hits = hits + jnp.where(spot == k * 128, tile, 0.0)
        local = top + jnp.log(jnp.sum(total, axis=1, keepdims=True))
        picked = jnp.sum(hits, axis=1, keepdims=True)
        values = jnp.where(place == 0, local, jnp.where(place == 1, picked, 0.0))
        for i in range(first, last):
            block_rows = values[(i - first) * own_tokens : (i - first + 1) * own_tokens]
            columns[rows_of((z + i + nz - half) % nz), :] = block_rows

    def summarize_all(first, last):
        for i in range(first, last, 3):
            summarize(i, min(i + 3, last))

    near_blocks = 2 * half + 1

    def before_far():
        target_work()
        summarize_all(0, near_blocks)

    def after_relay():
        send_targets()
        settle_early()

    early = list(waits)
    waits.clear()
    hooks = {2: after_relay, half: lambda: score(0, near_blocks), plus - 2: before_far}
    tree_gather(out_place, out_far_place, spread_send, spread_recv, hooks)
    score(near_blocks, nz)
    summarize_all(near_blocks, nz)

    turned = columns[...].T
    ngroup = tokens // 128
    for g in range(ngroup):
        stats[z, g : g + 1, :] = turned[0:1, g * 128 : (g + 1) * 128]
        stats[z, ngroup + g : ngroup + g + 1, :] = turned[1:2, g * 128 : (g + 1) * 128]

    for i in far_first_z:
        remote(stats.at[z], stats.at[z], stat_send, stat_recv, z_peer(i)).start()
    settle(waits)
    others = stats.at[0 : nz - 1]
    every = remote(others, others, stat_send, stat_recv, z_peer(1))
    every.wait_send()
    every.wait_recv()
    parts = [stats[i] for i in range(nz)]
    sums = [part[:ngroup] for part in parts]
    top = sums[0]
    for part in sums[1:]:
        top = jnp.maximum(top, part)
    total = add_up([jnp.exp(part - top) for part in sums])
    picked = add_up([part[ngroup:] for part in parts])
    lps[core * ndp + dp] = picked - (top + jnp.log(total))

    place = lps.at[core * ndp + dp]
    for step in far_first_dp + [0]:
        for turn in (0, 1):
            if step or turn:
                peer = ((x + step // SIDE) % SIDE) * SIDE + (y + step % SIDE) % SIDE
                device = (peer, z * 2 + (core + turn) % 2)
                remote(place, place, lp_send, lp_recv, device).start()
    others = lps.at[0 : 2 * ndp - 1]
    every = remote(others, others, lp_send, lp_recv, sibling)
    every.wait_recv()

    per_group = slots // ngroup
    taken = []
    for g in range(ngroup):
        hot = select[g * per_group * slots : (g + 1) * per_group * slots, :]
        between = lps[:ndp, g, :] - lps[ndp:, g, :]
        got = jnp.dot(hot, between, precision=HIGH, preferred_element_type=f32)
        row = lax.broadcasted_iota(jnp.int32, got.shape, 0) // slots
        lane = lax.broadcasted_iota(jnp.int32, got.shape, 1) // seq
        got = jnp.where(row == lane, got, 0.0)
        taken += [got[j * slots : (j + 1) * slots] for j in range(per_group)]
    fold = jnp.where(
        lax.broadcasted_iota(jnp.int32, (128, seq), 0) % seq
        == lax.broadcasted_iota(jnp.int32, (128, seq), 1),
        1.0,
        0.0,
    )
    moved = jnp.dot(add_up(taken), fold, precision=HIGH, preferred_element_type=f32)
    here = lax.broadcasted_iota(jnp.int32, (slots, slots), 0)
    there = lax.broadcasted_iota(jnp.int32, (slots, slots), 1)
    long = jnp.sum(jnp.where(here == there, lengths[...].astype(f32), 0.0), axis=1, keepdims=True)
    live = lax.broadcasted_iota(jnp.int32, (slots, seq), 1).astype(f32) < long
    kept = jnp.where(live, moved, 0.0)
    token_diff[...] = kept
    in_all = jnp.sum(kept, axis=1, keepdims=True)
    seq_diff[...] = jnp.sum(jnp.where(here == there, in_all, 0.0), axis=0, keepdims=True)

    every.wait_send()


def local(
    nz,
    hidden_policy,
    hidden_reference,
    ffn_gain_policy,
    ffn_gain_reference,
    up_policy,
    up_reference,
    down_policy,
    down_reference,
    final_gain_policy,
    final_gain_reference,
    out_policy,
    out_reference,
    move_plan,
    lengths,
    targets,
):
    slots, seq, part = hidden_policy.shape
    tokens = slots * seq
    width = up_policy.shape[0]
    units = up_policy.shape[1]
    vocab = out_policy.shape[1]
    ndp = SIDE * SIDE
    own = tokens // nz
    ngroup = tokens // 128
    plus = nz // 2
    any_space = pl.BlockSpec(memory_space=pl.ANY)
    vmem = pl.BlockSpec(memory_space=pltpu.VMEM)
    dma = pltpu.SemaphoreType.DMA
    ring = (2, plus, SUBS)
    token_diff, seq_diff = pl.pallas_call(
        functools.partial(kernel, nz),
        out_shape=(
            jax.ShapeDtypeStruct((slots, seq), f32),
            jax.ShapeDtypeStruct((1, slots), f32),
        ),
        in_specs=[any_space] * 15,
        out_specs=(vmem, vmem),
        scratch_shapes=[
            pltpu.VMEM((1, ndp * slots), jnp.int32),
            pltpu.VMEM((1, slots), jnp.int32),
            pltpu.VMEM((2, 1, width), f32),
            pltpu.VMEM((width // 128, own, 128), f32),
            pltpu.VMEM((2, tokens, part), bf16),
            pltpu.VMEM((width // 128, tokens, 128), bf16),
            pltpu.VMEM((tokens, width), bf16),
            pltpu.VMEM((width, 2 * units), bf16),
            pltpu.VMEM((2 * units, width), bf16),
            pltpu.VMEM((width, 2 * vocab), bf16),
            pltpu.VMEM((tokens, width), f32),
            pltpu.VMEM((2, plus, own, width), SUM_TYPE),
            pltpu.VMEM((2, plus, own, width), SUM_TYPE),
            pltpu.VMEM((tokens, width), bf16),
            pltpu.VMEM((tokens, 2 * vocab), f32),
            pltpu.VMEM((tokens, 128), f32),
            pltpu.VMEM((ndp, slots, seq), jnp.int32),
            pltpu.VMEM((tokens, 1), jnp.int32),
            pltpu.VMEM((tokens, ndp * slots), f32),
            pltpu.VMEM((slots * slots, ndp), f32),
            pltpu.VMEM((nz, 2 * ngroup, 128), f32),
            pltpu.VMEM((2 * ndp, ngroup, 128), f32),
            dma((9,)),
            dma((4,)),
            dma((4,)),
            dma(ring),
            dma(ring),
            dma(ring),
            dma(ring),
            dma(ring),
            dma(ring),
            dma((2, 2, 2)),
            dma((2, 2, 2)),
            dma((2, 4, 2, 2)),
            dma((2, 4, 2, 2)),
            dma,
            dma,
            dma,
            dma,
            dma,
            dma,
        ],
        compiler_params=pltpu.CompilerParams(
            collective_id=0, has_side_effects=True, vmem_limit_bytes=60 * 1024 * 1024
        ),
        name="score",
    )(
        hidden_policy.reshape(tokens, part),
        hidden_reference.reshape(tokens, part),
        ffn_gain_policy.reshape(1, width),
        ffn_gain_reference.reshape(1, width),
        up_policy,
        up_reference,
        down_policy,
        down_reference,
        final_gain_policy.reshape(1, width),
        final_gain_reference.reshape(1, width),
        out_policy,
        out_reference,
        move_plan.reshape(1, ndp * slots),
        lengths.reshape(1, slots),
        targets,
    )
    def hand_over(token_in, seq_in, token_out, seq_out):
        token_out[...] = token_in[...]
        seq_out[...] = seq_in[...]

    token_diff, seq_diff = pl.pallas_call(
        hand_over,
        out_shape=(
            jax.ShapeDtypeStruct((slots, seq), f32),
            jax.ShapeDtypeStruct((1, slots), f32),
        ),
        name="hand_over",
    )(token_diff, seq_diff)
    return token_diff, seq_diff.reshape(slots)


def solution(mesh):
    nz = mesh.shape["mp"] // 2
    return jax.shard_map(
        functools.partial(local, nz),
        mesh=mesh,
        in_specs=(
            P("dp", None, "mp"),
            P("dp", None, "mp"),
            P(),
            P(),
            P(None, "mp"),
            P(None, "mp"),
            P("mp", None),
            P("mp", None),
            P(),
            P(),
            P("dp", "mp"),
            P("dp", "mp"),
            P(),
            P("dp"),
            P("dp", None),
        ),
        out_specs=(P("dp", None), P("dp")),
        check_vma=False,
    )
```

```python
import functools

import jax
import jax.numpy as jnp
from jax import lax
from jax.experimental import pallas as pl
from jax.experimental.pallas import tpu as pltpu
from jax.sharding import PartitionSpec as P

MESH = pl.DeviceIdType.MESH
EPS = 1e-05
SIDE = 4
SUBS = 2
SUM_TYPE = jnp.bfloat16
HIGH = lax.Precision.HIGHEST
f32 = jnp.float32
bf16 = jnp.bfloat16


def remote(src, dst, send_sem, recv_sem, device):
    return pltpu.make_async_remote_copy(
        src_ref=src,
        dst_ref=dst,
        send_sem=send_sem,
        recv_sem=recv_sem,
        device_id=device,
        device_id_type=MESH,
    )


def add_up(parts):
    while len(parts) > 1:
        parts = [
            parts[i] + parts[i + 1] if i + 1 < len(parts) else parts[i]
            for i in range(0, len(parts), 2)
        ]
    return parts[0]


def normed_tiles(load, count, gain, width, store):
    center = jnp.sum(add_up([load(i) for i in range(count)]), axis=1, keepdims=True) / width
    squares = [jnp.square(load(i) - center) for i in range(count)]
    spread = jnp.sum(add_up(squares), axis=1, keepdims=True) / width
    scale = lax.rsqrt(spread + EPS)
    for i in range(count):
        tile = (load(i) - center) * scale * gain[:, i * 128 : (i + 1) * 128]
        store(i, tile.astype(bf16))


def kernel(
    nz,
    hidden_p,
    hidden_r,
    ffn_gain_p,
    ffn_gain_r,
    up_p,
    up_r,
    down_p,
    down_r,
    final_gain_p,
    final_gain_r,
    out_p,
    out_r,
    plan_hbm,
    lengths_hbm,
    targets,
    token_diff,
    seq_diff,
    plan_row,
    lengths,
    gains,
    after,
    halves,
    outbox,
    folded,
    feats,
    normed_in,
    up,
    down,
    out,
    partial,
    sums_out,
    sums_in,
    normed_out,
    logits,
    columns,
    wanted,
    target_col,
    slot_hot,
    select,
    stats,
    lps,
    local_sem,
    swap_send,
    swap_recv,
    gather_send,
    gather_recv,
    sum_send,
    sum_recv,
    spread_send,
    spread_recv,
    near_send,
    near_recv,
    far_send,
    far_recv,
    target_send,
    target_recv,
    stat_send,
    stat_recv,
    lp_send,
    lp_recv,
):
    dp = lax.axis_index("dp")
    mp = lax.axis_index("mp")
    z, core = mp // 2, mp % 2
    x, y = dp // SIDE, dp % SIDE
    ndp = SIDE * SIDE
    tokens, width = normed_out.shape
    slots, seq = token_diff.shape
    nfeat = width // 128
    own_tokens = tokens // nz
    units = up_p.shape[1]
    vocab = out_p.shape[1]
    depth = out_p.shape[0]
    piece = depth // 2
    quarter = piece // 2
    waits = []

    far_first_z = sorted(range(1, nz), key=lambda i: -min(i, nz - i))
    far_first_dp = sorted(
        range(1, ndp),
        key=lambda i: -min(i // SIDE, SIDE - i // SIDE) - min(i % SIDE, SIDE - i % SIDE),
    )

    def z_peer(step):
        return (dp, ((z + step + nz) % nz) * 2 + core)

    def xy_peer(axis, step):
        if axis == 0:
            return (((x + step + SIDE) % SIDE) * SIDE + y, mp)
        return (x * SIDE + (y + step + SIDE) % SIDE, mp)

    sibling = (dp, z * 2 + 1 - core)

    def send(copy):
        copy.start()
        waits.append(copy)

    def settle(copies):
        for copy in copies:
            copy.wait_send()
        copies.clear()

    own_rows = pl.ds(pl.multiple_of(dp * depth, depth), depth)

    def places(c):
        return (
            folded.at[z, c],
            out.at[own_rows, c * vocab : (c + 1) * vocab],
            up.at[:, c * units : (c + 1) * units],
            down.at[c * units : (c + 1) * units, :],
        )

    policy = (hidden_p, out_p, up_p, down_p, ffn_gain_p, final_gain_p)
    refer = (hidden_r, out_r, up_r, down_r, ffn_gain_r, final_gain_r)

    def local_copy(c, i):
        mine = policy if c == 0 else refer
        place = halves.at[0] if i == 0 else gains.at[i - 4] if i >= 4 else places(c)[i]
        return pltpu.make_async_copy(mine[i], place, local_sem.at[i])

    def other_copy(c):
        theirs = refer if c == 0 else policy
        return pltpu.make_async_copy(theirs[0], halves.at[1], local_sem.at[9])

    small_copies = [
        pltpu.make_async_copy(plan_hbm, plan_row, local_sem.at[6]),
        pltpu.make_async_copy(lengths_hbm, lengths, local_sem.at[7]),
        pltpu.make_async_copy(targets, wanted.at[dp], local_sem.at[8]),
    ]
    for c in (0, 1):

        @pl.when(core == c)
        def _(c=c):
            other_copy(c).start()
            for i in range(6):
                local_copy(c, i).start()

    for copy in small_copies:
        copy.start()

    barrier = pltpu.get_barrier_semaphore()
    greeted = [sibling] + [z_peer(step) for step in (1, -1, 2, -2)]
    greeted += [xy_peer(axis, step) for axis in (0, 1) for step in (1, -1)]
    for device in greeted:
        pl.semaphore_signal(barrier, inc=1, device_id=device, device_id_type=MESH)
    for c in (0, 1):

        @pl.when(core == c)
        def _(c=c):
            local_copy(c, 0).wait()
            other_copy(c).wait()

    def fold(i):
        half_tokens = tokens // 2
        return jnp.concatenate([halves[i, :half_tokens, :], halves[i, half_tokens:, :]], axis=1)

    outbox[...] = fold(1)
    folded[z, core] = fold(0)
    pl.semaphore_wait(barrier, len(greeted))

    for c in (0, 1):

        @pl.when(core == c)
        def _(c=c):
            remote(outbox, places(c)[0], swap_send.at[0], swap_recv.at[0], sibling).start()

    def swap_wait(i):
        for c in (0, 1):

            @pl.when(core == c)
            def _(c=c):
                theirs = refer if c == 0 else policy
                remote(
                    theirs[i] if i else outbox, places(1 - c)[i], swap_send.at[i], swap_recv.at[i], sibling
                ).wait_recv()
                if i:
                    local_copy(c, i).wait()

    def swap_done(i):
        for c in (0, 1):

            @pl.when(core == c)
            def _(c=c):
                theirs = refer if c == 0 else policy
                remote(
                    theirs[i] if i else outbox, places(c)[i], swap_send.at[i], swap_recv.at[i], sibling
                ).wait_send()

    plus, minus = nz // 2, nz // 2 - 1

    half = plus // 2
    ways = ((0, 1), (1, -1))

    def reach(way, sub):
        return plus if (sub < (SUBS + 1) // 2) == (way == 0) else minus

    def tree_gather(place, far_place, send_sem, recv_sem, hooks, between=None):
        def arrived(way, step, t, sub):
            block = place(step, t, sub)
            sems = send_sem.at[way, t - 1, sub], recv_sem.at[way, t - 1, sub]
            remote(block, block, *sems, z_peer(step)).wait_recv()

        def wait_odd(first, last):
            for t in range(first, last, 2):
                for sub in range(SUBS):
                    for way, step in ways:
                        if t <= reach(way, sub):
                            arrived(way, step, t, sub)

        for held in range(0, plus + 1, 2):
            late = []
            for sub in range(SUBS):
                if held == 0 and sub == 1 and between is not None:
                    for copy in late:
                        send(copy)
                    late = []
                    between()
                for way, step in ways:
                    hops = reach(way, sub)
                    if 0 < held <= hops:
                        arrived(way, step, held, sub)
                    for far in (2, 1):
                        t = held + far
                        if t <= hops:
                            sems = send_sem.at[way, t - 1, sub], recv_sem.at[way, t - 1, sub]
                            block = place(step, held, sub)
                            there = far_place(step, held, t, sub)
                            copy = remote(block, there, *sems, z_peer(step * far))
                            if far == 1:
                                late.append(copy)
                            else:
                                send(copy)
            for copy in late:
                send(copy)
            if held == half:
                wait_odd(1, half)
            if held in hooks:
                hooks[held]()
        wait_odd(half + 1, plus + 1)

    def block_rows(h, along, across, part):
        first, second = (along, across) if h == 0 else (across, along)
        start = (first * SIDE + second) * depth + h * piece
        if part is None:
            return out.at[pl.ds(pl.multiple_of(start, piece), piece), :]
        return out.at[pl.ds(pl.multiple_of(start + part * quarter, quarter), quarter), :]

    def place_of(h):
        return (x, y) if h == 0 else (y, x)

    def along_of(h, j):
        return (place_of(h)[0] + (0, -1, 1, 2)[j] + SIDE) % SIDE

    def near(h, way, forward):
        step = (1, -1)[way]
        u, v = place_of(h)
        if forward:
            rows = block_rows(h, (u - step + SIDE) % SIDE, v, way)
        else:
            rows = block_rows(h, u, v, None)
        sem = (h, way, int(forward))
        return remote(rows, rows, near_send.at[sem], near_recv.at[sem], xy_peer(h, step))

    def near_wait(h, way, forward):
        step = (1, -1)[way]
        u, v = place_of(h)
        if forward:
            rows = block_rows(h, (u - 2 * step + SIDE) % SIDE, v, way)
        else:
            rows = block_rows(h, (u - step + SIDE) % SIDE, v, None)
        sem = (h, way, int(forward))
        remote(rows, rows, near_send.at[sem], near_recv.at[sem], xy_peer(h, step)).wait_recv()

    def far(h, j, way, forward):
        step = (1, -1)[way]
        v = place_of(h)[1]
        if forward:
            rows = block_rows(h, along_of(h, j), (v - step + SIDE) % SIDE, way)
        else:
            rows = block_rows(h, along_of(h, j), v, None)
        sem = (h, j, way, int(forward))
        return remote(rows, rows, far_send.at[sem], far_recv.at[sem], xy_peer(1 - h, step))

    def far_wait(h, j, way, forward):
        step = (1, -1)[way]
        v = place_of(h)[1]
        if forward:
            rows = block_rows(h, along_of(h, j), (v - 2 * step + SIDE) % SIDE, way)
        else:
            rows = block_rows(h, along_of(h, j), (v - step + SIDE) % SIDE, None)
        sem = (h, j, way, int(forward))
        remote(rows, rows, far_send.at[sem], far_recv.at[sem], xy_peer(1 - h, step)).wait_recv()

    both = [(h, way) for h in (0, 1) for way in (0, 1)]

    def out_round_0():
        swap_wait(1)
        for h, way in both:
            send(near(h, way, False))
        for h, way in both:
            send(far(h, 0, way, False))

    def out_round_1():
        for h, way in both:
            near_wait(h, way, False)
            send(near(h, way, True))
        for j in (1, 2):
            for h, way in both:
                send(far(h, j, way, False))
        for h, way in both:
            far_wait(h, 0, way, False)
            send(far(h, 0, way, True))

    def out_round_2():
        for h, way in both:
            near_wait(h, way, True)
        for h, way in both:
            send(far(h, 3, way, False))
        for j in (1, 2):
            for h, way in both:
                far_wait(h, j, way, False)
                send(far(h, j, way, True))

    def out_round_3():
        for h, way in both:
            far_wait(h, 3, way, False)
            send(far(h, 3, way, True))

    def out_round_4():
        for j in range(4):
            for h, way in both:
                far_wait(h, j, way, True)

    def other_half():
        swap_wait(0)

    def feat_place(step, t, sub):
        return folded.at[(z - step * t + nz) % nz, (core + sub) % 2]

    def feat_far_place(step, held, t, sub):
        return feat_place(step, held, sub)

    def unfold(first, last):
        part = halves.shape[2]
        half_tokens = tokens // 2
        for t in range(first, last):
            for step in (1, -1):
                if t <= (plus if step == 1 else minus) and (t or step == 1):
                    source = (z - step * t + nz) % nz
                    sides = [folded[source, c] for c in (0, 1)]
                    for i in (0, 1):
                        feats[source, i * half_tokens : (i + 1) * half_tokens, :] = jnp.concatenate(
                            [side[:, i * part : (i + 1) * part] for side in sides], axis=1
                        )

    def whole_order(row):
        block = (row // own_tokens + (z + nz - half)) % nz
        return block * own_tokens + row % own_tokens

    def index_work():
        for copy in small_copies:
            copy.wait()
        request = lax.broadcasted_iota(jnp.int32, (slots, ndp * slots), 1)
        order = lax.broadcasted_iota(jnp.int32, (slots, ndp * slots), 0)
        spread_plan = jnp.where(request % slots == order, plan_row[...], 0).astype(bf16)
        request = lax.broadcasted_iota(jnp.int32, (ndp * slots, ndp), 0)
        holder = lax.broadcasted_iota(jnp.int32, (ndp * slots, ndp), 1)
        owner = jnp.where(request // slots == holder, 1.0, 0.0).astype(bf16)
        plan = jnp.dot(spread_plan, owner, preferred_element_type=f32)
        slot_id = lax.broadcasted_iota(jnp.int32, (slots, slots, ndp), 1) + dp * slots
        hot = jnp.broadcast_to(plan[:, None, :], (slots, slots, ndp)) == slot_id.astype(f32)
        select[...] = jnp.where(hot, 1.0, 0.0).reshape(slots * slots, ndp)
        token = lax.broadcasted_iota(jnp.int32, (tokens, ndp * slots), 0)
        lane = lax.broadcasted_iota(jnp.int32, (tokens, ndp * slots), 1)
        own_request = lane == dp * slots + whole_order(token) // seq
        owner_slot = jnp.sum(
            jnp.where(own_request, plan_row[...].astype(f32), 0.0), axis=1, keepdims=True
        )
        slot_hot[...] = jnp.where(lane.astype(f32) == owner_slot, 1.0, 0.0)

    def first_hook():
        for c in (0, 1):

            @pl.when(core == c)
            def _(c=c):
                theirs = refer if c == 0 else policy
                for i, place in enumerate(places(c)):
                    if i:
                        remote(theirs[i], place, swap_send.at[i], swap_recv.at[i], sibling).start()

        out_round_0()
        index_work()

    hooks = {0: first_hook, half: lambda: unfold(0, half + 1), plus - 2: out_round_1}
    tree_gather(feat_place, feat_far_place, gather_send, gather_recv, hooks, other_half)
    unfold(half + 1, plus + 1)

    for i in (4, 5):
        for c in (0, 1):

            @pl.when(core == c)
            def _(c=c, i=i):
                local_copy(c, i).wait()

    row_step = min(64, tokens)

    @pl.loop(0, tokens // row_step)
    def _(i):
        rows = pl.ds(pl.multiple_of(i * row_step, row_step), row_step)

        def store(k, tile):
            normed_in[rows, k * 128 : (k + 1) * 128] = tile

        normed_tiles(lambda k: feats[k, rows, :].astype(f32), nfeat, gains[0], width, store)

    swap_wait(2)
    swap_wait(3)
    pre = jnp.dot(normed_in[...], up[...], preferred_element_type=f32)
    active = jax.nn.gelu(pre).astype(bf16)

    sub_width = width // SUBS

    def rows_of(chunk):
        return pl.ds(pl.multiple_of(chunk * own_tokens, own_tokens), own_tokens)

    def sum_copy(way, t, sub):
        cols = slice(sub * sub_width, (sub + 1) * sub_width)
        return remote(
            sums_out.at[way, t - 1, :, cols],
            sums_in.at[way, t - 1, :, cols],
            sum_send.at[way, t - 1, sub],
            sum_recv.at[way, t - 1, sub],
            z_peer((1, -1)[way] * (1 if t % 2 else 2)),
        )

    def hand_on(t):
        for sub in range(SUBS):
            cols = slice(sub * sub_width, (sub + 1) * sub_width)
            if t == plus:
                partial[:, cols] = jnp.dot(active, down[:, cols], preferred_element_type=f32)
            for way, step in ways:
                hops = reach(way, sub)
                if t > hops:
                    continue
                term = partial[rows_of((z + step * t + nz) % nz), cols]
                if t % 2 == 0:
                    for behind in (t + 2, t + 1):
                        if behind <= hops:
                            sum_copy(way, behind, sub).wait_recv()
                            term = term + sums_in[way, behind - 1, :, cols].astype(f32)
                sums_out[way, t - 1, :, cols] = term.astype(sums_out.dtype)
                send(sum_copy(way, t, sub))

    hand_on(plus)
    hand_on(plus - 1)
    for t in range(plus - 2, 0, -2):
        hand_on(t - 1)
        hand_on(t)
        if t == plus - 2:
            out_round_2()
    for t in (1, 2):
        for sub in range(SUBS):
            for way in (0, 1):
                sum_copy(way, t, sub).wait_recv()

    mine = rows_of(z)
    for k in range(nfeat):
        cols = slice(k * 128, (k + 1) * 128)
        came = [sums_in[way, t, :, cols].astype(f32) for way in (0, 1) for t in (0, 1)]
        total = partial[mine, cols] + add_up(came)
        after[k] = feats[k, mine, :].astype(f32) + total

    def store_out(k, tile):
        normed_out[half * own_tokens : (half + 1) * own_tokens, k * 128 : (k + 1) * 128] = tile

    normed_tiles(lambda k: after[k], nfeat, gains[1], width, store_out)

    def out_place(step, t, sub):
        slot = (half - step * t + nz) % nz
        cols = slice(sub * sub_width, (sub + 1) * sub_width)
        return normed_out.at[slot * own_tokens : (slot + 1) * own_tokens, cols]

    def out_far_place(step, held, t, sub):
        return out_place(step, t, sub)

    def target_copy(i, source):
        return remote(
            wanted.at[source],
            wanted.at[source],
            target_send,
            target_recv,
            ((dp + i) % ndp, mp),
        )

    def send_targets():
        out_round_4()
        for i in range(1, ndp):
            target_copy(i, dp).start()

    def settle_early():
        for i in range(4):
            swap_done(i)
        settle(early)

    def target_work():
        others = wanted.at[0 : ndp - 1]
        every = remote(others, others, target_send, target_recv, sibling)
        every.wait_send()
        every.wait_recv()
        all_targets = wanted[...].astype(f32).reshape(ndp * slots, seq)
        seen = jnp.dot(slot_hot[...], all_targets, precision=HIGH, preferred_element_type=f32)
        position = lax.broadcasted_iota(jnp.int32, (tokens, seq), 1)
        row = lax.broadcasted_iota(jnp.int32, (tokens, seq), 0)
        target_col[...] = jnp.sum(
            jnp.where(position == whole_order(row) % seq, seen, 0.0), axis=1, keepdims=True
        ).astype(jnp.int32)

    block = 256
    ntile = 2 * vocab // 128

    def score(first, last):
        rows = slice(first * own_tokens, last * own_tokens)

        @pl.loop(0, 2 * vocab // block)
        def _(i):
            cols = pl.ds(pl.multiple_of(i * block, block), block)
            logits[rows, cols] = jnp.dot(
                normed_out[rows, :], out[:, cols], preferred_element_type=f32
            )

    def summarize(first, last):
        rows = slice(first * own_tokens, last * own_tokens)
        shape = ((last - first) * own_tokens, 128)

        def load(k):
            return logits[rows, k * 128 : (k + 1) * 128]

        top = load(0)
        for k in range(1, ntile):
            top = jnp.maximum(top, load(k))
        top = jnp.max(top, axis=1, keepdims=True)
        place = lax.broadcasted_iota(jnp.int32, shape, 1)
        spot = target_col[rows, :] - z * (2 * vocab) - place
        total = jnp.zeros(shape, f32)
        hits = jnp.zeros(shape, f32)
        for k in range(ntile):
            tile = load(k)
            total = total + jnp.exp(tile - top)
            hits = hits + jnp.where(spot == k * 128, tile, 0.0)
        local = top + jnp.log(jnp.sum(total, axis=1, keepdims=True))
        picked = jnp.sum(hits, axis=1, keepdims=True)
        values = jnp.where(place == 0, local, jnp.where(place == 1, picked, 0.0))
        for i in range(first, last):
            block_rows = values[(i - first) * own_tokens : (i - first + 1) * own_tokens]
            columns[rows_of((z + i + nz - half) % nz), :] = block_rows

    def summarize_all(first, last):
        for i in range(first, last, 3):
            summarize(i, min(i + 3, last))

    near_blocks = 2 * half + 1

    def before_far():
        target_work()
        summarize_all(0, near_blocks)

    def after_relay():
        send_targets()
        settle_early()

    early = list(waits)
    waits.clear()
    hooks = {
        0: out_round_3,
        2: after_relay,
        half: lambda: score(0, near_blocks),
        plus - 2: before_far,
    }
    tree_gather(out_place, out_far_place, spread_send, spread_recv, hooks)
    score(near_blocks, nz)
    summarize_all(near_blocks, nz)

    turned = columns[...].T
    ngroup = tokens // 128
    for g in range(ngroup):
        stats[z, g : g + 1, :] = turned[0:1, g * 128 : (g + 1) * 128]
        stats[z, ngroup + g : ngroup + g + 1, :] = turned[1:2, g * 128 : (g + 1) * 128]

    for i in far_first_z:
        remote(stats.at[z], stats.at[z], stat_send, stat_recv, z_peer(i)).start()
    settle(waits)
    others = stats.at[0 : nz - 1]
    every = remote(others, others, stat_send, stat_recv, z_peer(1))
    every.wait_send()
    every.wait_recv()
    parts = [stats[i] for i in range(nz)]
    sums = [part[:ngroup] for part in parts]
    top = sums[0]
    for part in sums[1:]:
        top = jnp.maximum(top, part)
    total = add_up([jnp.exp(part - top) for part in sums])
    picked = add_up([part[ngroup:] for part in parts])
    lps[core * ndp + dp] = picked - (top + jnp.log(total))

    place = lps.at[core * ndp + dp]
    for step in far_first_dp + [0]:
        for turn in (0, 1):
            if step or turn:
                peer = ((x + step // SIDE) % SIDE) * SIDE + (y + step % SIDE) % SIDE
                device = (peer, z * 2 + (core + turn) % 2)
                remote(place, place, lp_send, lp_recv, device).start()
    others = lps.at[0 : 2 * ndp - 1]
    every = remote(others, others, lp_send, lp_recv, sibling)
    every.wait_recv()

    per_group = slots // ngroup
    taken = []
    for g in range(ngroup):
        hot = select[g * per_group * slots : (g + 1) * per_group * slots, :]
        between = lps[:ndp, g, :] - lps[ndp:, g, :]
        got = jnp.dot(hot, between, precision=HIGH, preferred_element_type=f32)
        row = lax.broadcasted_iota(jnp.int32, got.shape, 0) // slots
        lane = lax.broadcasted_iota(jnp.int32, got.shape, 1) // seq
        got = jnp.where(row == lane, got, 0.0)
        taken += [got[j * slots : (j + 1) * slots] for j in range(per_group)]
    fold = jnp.where(
        lax.broadcasted_iota(jnp.int32, (128, seq), 0) % seq
        == lax.broadcasted_iota(jnp.int32, (128, seq), 1),
        1.0,
        0.0,
    )
    moved = jnp.dot(add_up(taken), fold, precision=HIGH, preferred_element_type=f32)
    here = lax.broadcasted_iota(jnp.int32, (slots, slots), 0)
    there = lax.broadcasted_iota(jnp.int32, (slots, slots), 1)
    long = jnp.sum(jnp.where(here == there, lengths[...].astype(f32), 0.0), axis=1, keepdims=True)
    live = lax.broadcasted_iota(jnp.int32, (slots, seq), 1).astype(f32) < long
    kept = jnp.where(live, moved, 0.0)
    token_diff[...] = kept
    in_all = jnp.sum(kept, axis=1, keepdims=True)
    seq_diff[...] = jnp.sum(jnp.where(here == there, in_all, 0.0), axis=0, keepdims=True)

    every.wait_send()


def local(
    nz,
    hidden_policy,
    hidden_reference,
    ffn_gain_policy,
    ffn_gain_reference,
    up_policy,
    up_reference,
    down_policy,
    down_reference,
    final_gain_policy,
    final_gain_reference,
    out_policy,
    out_reference,
    move_plan,
    lengths,
    targets,
):
    slots, seq, part = hidden_policy.shape
    tokens = slots * seq
    width = up_policy.shape[0]
    units = up_policy.shape[1]
    vocab = out_policy.shape[1]
    ndp = SIDE * SIDE
    own = tokens // nz
    ngroup = tokens // 128
    plus = nz // 2
    any_space = pl.BlockSpec(memory_space=pl.ANY)
    vmem = pl.BlockSpec(memory_space=pltpu.VMEM)
    dma = pltpu.SemaphoreType.DMA
    ring = (2, plus, SUBS)
    token_diff, seq_diff = pl.pallas_call(
        functools.partial(kernel, nz),
        out_shape=(
            jax.ShapeDtypeStruct((slots, seq), f32),
            jax.ShapeDtypeStruct((1, slots), f32),
        ),
        in_specs=[any_space] * 15,
        out_specs=(vmem, vmem),
        scratch_shapes=[
            pltpu.VMEM((1, ndp * slots), jnp.int32),
            pltpu.VMEM((1, slots), jnp.int32),
            pltpu.VMEM((2, 1, width), f32),
            pltpu.VMEM((width // 128, own, 128), f32),
            pltpu.VMEM((2, tokens, part), bf16),
            pltpu.VMEM((tokens // 2, 2 * part), bf16),
            pltpu.VMEM((nz, 2, tokens // 2, 128), bf16),
            pltpu.VMEM((width // 128, tokens, 128), bf16),
            pltpu.VMEM((tokens, width), bf16),
            pltpu.VMEM((width, 2 * units), bf16),
            pltpu.VMEM((2 * units, width), bf16),
            pltpu.VMEM((width, 2 * vocab), bf16),
            pltpu.VMEM((tokens, width), f32),
            pltpu.VMEM((2, plus, own, width), SUM_TYPE),
            pltpu.VMEM((2, plus, own, width), SUM_TYPE),
            pltpu.VMEM((tokens, width), bf16),
            pltpu.VMEM((tokens, 2 * vocab), f32),
            pltpu.VMEM((tokens, 128), f32),
            pltpu.VMEM((ndp, slots, seq), jnp.int32),
            pltpu.VMEM((tokens, 1), jnp.int32),
            pltpu.VMEM((tokens, ndp * slots), f32),
            pltpu.VMEM((slots * slots, ndp), f32),
            pltpu.VMEM((nz, 2 * ngroup, 128), f32),
            pltpu.VMEM((2 * ndp, ngroup, 128), f32),
            dma((10,)),
            dma((4,)),
            dma((4,)),
            dma(ring),
            dma(ring),
            dma(ring),
            dma(ring),
            dma(ring),
            dma(ring),
            dma((2, 2, 2)),
            dma((2, 2, 2)),
            dma((2, 4, 2, 2)),
            dma((2, 4, 2, 2)),
            dma,
            dma,
            dma,
            dma,
            dma,
            dma,
        ],
        compiler_params=pltpu.CompilerParams(
            collective_id=0, has_side_effects=True, vmem_limit_bytes=60 * 1024 * 1024
        ),
        name="score",
    )(
        hidden_policy.reshape(tokens, part),
        hidden_reference.reshape(tokens, part),
        ffn_gain_policy.reshape(1, width),
        ffn_gain_reference.reshape(1, width),
        up_policy,
        up_reference,
        down_policy,
        down_reference,
        final_gain_policy.reshape(1, width),
        final_gain_reference.reshape(1, width),
        out_policy,
        out_reference,
        move_plan.reshape(1, ndp * slots),
        lengths.reshape(1, slots),
        targets,
    )
    def hand_over(token_in, seq_in, token_out, seq_out):
        token_out[...] = token_in[...]
        seq_out[...] = seq_in[...]

    token_diff, seq_diff = pl.pallas_call(
        hand_over,
        out_shape=(
            jax.ShapeDtypeStruct((slots, seq), f32),
            jax.ShapeDtypeStruct((1, slots), f32),
        ),
        name="hand_over",
    )(token_diff, seq_diff)
    return token_diff, seq_diff.reshape(slots)


def solution(mesh):
    nz = mesh.shape["mp"] // 2
    return jax.shard_map(
        functools.partial(local, nz),
        mesh=mesh,
        in_specs=(
            P("dp", None, "mp"),
            P("dp", None, "mp"),
            P(),
            P(),
            P(None, "mp"),
            P(None, "mp"),
            P("mp", None),
            P("mp", None),
            P(),
            P(),
            P("dp", "mp"),
            P("dp", "mp"),
            P(),
            P("dp"),
            P("dp", None),
        ),
        out_specs=(P("dp", None), P("dp")),
        check_vma=False,
    )
```

```python
import functools

import jax
import jax.numpy as jnp
from jax import lax
from jax.experimental import pallas as pl
from jax.experimental.pallas import tpu as pltpu
from jax.sharding import PartitionSpec as P

MESH = pl.DeviceIdType.MESH
EPS = 1e-05
SIDE = 4
SUBS = 2
SUM_TYPE = jnp.bfloat16
HIGH = lax.Precision.HIGHEST
f32 = jnp.float32
bf16 = jnp.bfloat16


def remote(src, dst, send_sem, recv_sem, device):
    return pltpu.make_async_remote_copy(
        src_ref=src,
        dst_ref=dst,
        send_sem=send_sem,
        recv_sem=recv_sem,
        device_id=device,
        device_id_type=MESH,
    )


def add_up(parts):
    while len(parts) > 1:
        parts = [
            parts[i] + parts[i + 1] if i + 1 < len(parts) else parts[i]
            for i in range(0, len(parts), 2)
        ]
    return parts[0]


def normed_tiles(load, count, gain, width, store):
    center = jnp.sum(add_up([load(i) for i in range(count)]), axis=1, keepdims=True) / width
    squares = [jnp.square(load(i) - center) for i in range(count)]
    spread = jnp.sum(add_up(squares), axis=1, keepdims=True) / width
    scale = lax.rsqrt(spread + EPS)
    for i in range(count):
        tile = (load(i) - center) * scale * gain[:, i * 128 : (i + 1) * 128]
        store(i, tile.astype(bf16))


def kernel(
    nz,
    hidden_p,
    hidden_r,
    ffn_gain_p,
    ffn_gain_r,
    up_p,
    up_r,
    down_p,
    down_r,
    final_gain_p,
    final_gain_r,
    out_p,
    out_r,
    plan_hbm,
    lengths_hbm,
    targets,
    token_diff,
    seq_diff,
    plan_row,
    lengths,
    gains,
    after,
    halves,
    outbox,
    folded,
    feats,
    normed_in,
    up,
    down,
    out,
    partial,
    sums_out,
    sums_in,
    normed_out,
    logits,
    columns,
    wanted,
    target_col,
    slot_hot,
    select,
    stats,
    lps,
    local_sem,
    swap_send,
    swap_recv,
    gather_send,
    gather_recv,
    sum_send,
    sum_recv,
    spread_send,
    spread_recv,
    near_send,
    near_recv,
    far_send,
    far_recv,
    target_send,
    target_recv,
    stat_send,
    stat_recv,
    lp_send,
    lp_recv,
):
    dp = lax.axis_index("dp")
    mp = lax.axis_index("mp")
    z, core = mp // 2, mp % 2
    x, y = dp // SIDE, dp % SIDE
    ndp = SIDE * SIDE
    tokens, width = normed_out.shape
    slots, seq = token_diff.shape
    nfeat = width // 128
    own_tokens = tokens // nz
    units = up_p.shape[1]
    vocab = out_p.shape[1]
    depth = out_p.shape[0]
    piece = depth // 2
    quarter = piece // 2
    waits = []

    far_first_z = sorted(range(1, nz), key=lambda i: -min(i, nz - i))
    far_first_dp = sorted(
        range(1, ndp),
        key=lambda i: -min(i // SIDE, SIDE - i // SIDE) - min(i % SIDE, SIDE - i % SIDE),
    )

    def z_peer(step):
        return (dp, ((z + step + nz) % nz) * 2 + core)

    def xy_peer(axis, step):
        if axis == 0:
            return (((x + step + SIDE) % SIDE) * SIDE + y, mp)
        return (x * SIDE + (y + step + SIDE) % SIDE, mp)

    sibling = (dp, z * 2 + 1 - core)

    def send(copy):
        copy.start()
        waits.append(copy)

    def settle(copies):
        for copy in copies:
            copy.wait_send()
        copies.clear()

    own_rows = pl.ds(pl.multiple_of(dp * depth, depth), depth)

    def places(c):
        return (
            folded.at[z, c],
            out.at[own_rows, c * vocab : (c + 1) * vocab],
            up.at[:, c * units : (c + 1) * units],
            down.at[c * units : (c + 1) * units, :],
        )

    policy = (hidden_p, out_p, up_p, down_p, ffn_gain_p, final_gain_p)
    refer = (hidden_r, out_r, up_r, down_r, ffn_gain_r, final_gain_r)

    def local_copy(c, i):
        mine = policy if c == 0 else refer
        place = halves.at[0] if i == 0 else gains.at[i - 4] if i >= 4 else places(c)[i]
        return pltpu.make_async_copy(mine[i], place, local_sem.at[i])

    def other_copy(c):
        theirs = refer if c == 0 else policy
        return pltpu.make_async_copy(theirs[0], halves.at[1], local_sem.at[9])

    small_copies = [
        pltpu.make_async_copy(plan_hbm, plan_row, local_sem.at[6]),
        pltpu.make_async_copy(lengths_hbm, lengths, local_sem.at[7]),
        pltpu.make_async_copy(targets, wanted.at[dp], local_sem.at[8]),
    ]
    for c in (0, 1):

        @pl.when(core == c)
        def _(c=c):
            other_copy(c).start()
            for i in range(6):
                local_copy(c, i).start()

    for copy in small_copies:
        copy.start()

    barrier = pltpu.get_barrier_semaphore()
    greeted = [sibling] + [z_peer(step) for step in (1, -1, 2, -2)]
    greeted += [xy_peer(axis, step) for axis in (0, 1) for step in (1, -1)]
    for device in greeted:
        pl.semaphore_signal(barrier, inc=1, device_id=device, device_id_type=MESH)
    for c in (0, 1):

        @pl.when(core == c)
        def _(c=c):
            local_copy(c, 0).wait()
            other_copy(c).wait()

    def fold(i):
        half_tokens = tokens // 2
        return jnp.concatenate([halves[i, :half_tokens, :], halves[i, half_tokens:, :]], axis=1)

    outbox[...] = fold(1)
    folded[z, core] = fold(0)
    pl.semaphore_wait(barrier, len(greeted))

    for c in (0, 1):

        @pl.when(core == c)
        def _(c=c):
            remote(outbox, places(c)[0], swap_send.at[0], swap_recv.at[0], sibling).start()

    def swap_wait(i):
        for c in (0, 1):

            @pl.when(core == c)
            def _(c=c):
                theirs = refer if c == 0 else policy
                remote(
                    theirs[i] if i else outbox, places(1 - c)[i], swap_send.at[i], swap_recv.at[i], sibling
                ).wait_recv()
                if i:
                    local_copy(c, i).wait()

    def swap_done(i):
        for c in (0, 1):

            @pl.when(core == c)
            def _(c=c):
                theirs = refer if c == 0 else policy
                remote(
                    theirs[i] if i else outbox, places(c)[i], swap_send.at[i], swap_recv.at[i], sibling
                ).wait_send()

    plus, minus = nz // 2, nz // 2 - 1

    half = plus // 2
    ways = ((0, 1), (1, -1))

    def reach(way, sub):
        return plus if (sub < (SUBS + 1) // 2) == (way == 0) else minus

    def tree_gather(place, far_place, send_sem, recv_sem, hooks, between=None):
        def arrived(way, step, t, sub):
            block = place(step, t, sub)
            sems = send_sem.at[way, t - 1, sub], recv_sem.at[way, t - 1, sub]
            remote(block, block, *sems, z_peer(step)).wait_recv()

        def wait_odd(first, last):
            for t in range(first, last, 2):
                for sub in range(SUBS):
                    for way, step in ways:
                        if t <= reach(way, sub):
                            arrived(way, step, t, sub)

        for held in range(0, plus + 1, 2):
            late = []
            for sub in range(SUBS):
                if held == 0 and sub == 1 and between is not None:
                    for copy in late:
                        send(copy)
                    late = []
                    between()
                for way, step in ways:
                    hops = reach(way, sub)
                    if 0 < held <= hops:
                        arrived(way, step, held, sub)
                    for far in (2, 1):
                        t = held + far
                        if t <= hops:
                            sems = send_sem.at[way, t - 1, sub], recv_sem.at[way, t - 1, sub]
                            block = place(step, held, sub)
                            there = far_place(step, held, t, sub)
                            copy = remote(block, there, *sems, z_peer(step * far))
                            if far == 1:
                                late.append(copy)
                            else:
                                send(copy)
            for copy in late:
                send(copy)
            if held == half:
                wait_odd(1, half)
            if held in hooks:
                hooks[held]()
        wait_odd(half + 1, plus + 1)

    def block_rows(h, along, across, part):
        first, second = (along, across) if h == 0 else (across, along)
        start = (first * SIDE + second) * depth + h * piece
        if part is None:
            return out.at[pl.ds(pl.multiple_of(start, piece), piece), :]
        return out.at[pl.ds(pl.multiple_of(start + part * quarter, quarter), quarter), :]

    def place_of(h):
        return (x, y) if h == 0 else (y, x)

    def along_of(h, j):
        return (place_of(h)[0] + (0, -1, 1, 2)[j] + SIDE) % SIDE

    def near(h, way, forward):
        step = (1, -1)[way]
        u, v = place_of(h)
        if forward:
            rows = block_rows(h, (u - step + SIDE) % SIDE, v, way)
        else:
            rows = block_rows(h, u, v, None)
        sem = (h, way, int(forward))
        return remote(rows, rows, near_send.at[sem], near_recv.at[sem], xy_peer(h, step))

    def near_wait(h, way, forward):
        step = (1, -1)[way]
        u, v = place_of(h)
        if forward:
            rows = block_rows(h, (u - 2 * step + SIDE) % SIDE, v, way)
        else:
            rows = block_rows(h, (u - step + SIDE) % SIDE, v, None)
        sem = (h, way, int(forward))
        remote(rows, rows, near_send.at[sem], near_recv.at[sem], xy_peer(h, step)).wait_recv()

    def far(h, j, way, forward):
        step = (1, -1)[way]
        v = place_of(h)[1]
        if forward:
            rows = block_rows(h, along_of(h, j), (v - step + SIDE) % SIDE, way)
        else:
            rows = block_rows(h, along_of(h, j), v, None)
        sem = (h, j, way, int(forward))
        return remote(rows, rows, far_send.at[sem], far_recv.at[sem], xy_peer(1 - h, step))

    def far_wait(h, j, way, forward):
        step = (1, -1)[way]
        v = place_of(h)[1]
        if forward:
            rows = block_rows(h, along_of(h, j), (v - 2 * step + SIDE) % SIDE, way)
        else:
            rows = block_rows(h, along_of(h, j), (v - step + SIDE) % SIDE, None)
        sem = (h, j, way, int(forward))
        remote(rows, rows, far_send.at[sem], far_recv.at[sem], xy_peer(1 - h, step)).wait_recv()

    both = [(h, way) for h in (0, 1) for way in (0, 1)]

    def out_round_0():
        swap_wait(1)
        for h, way in both:
            send(near(h, way, False))
        for h, way in both:
            send(far(h, 0, way, False))

    def out_round_1():
        for h, way in both:
            near_wait(h, way, False)
            send(near(h, way, True))
        for j in (1, 2):
            for h, way in both:
                send(far(h, j, way, False))
        for h, way in both:
            far_wait(h, 0, way, False)
            send(far(h, 0, way, True))

    def out_round_2():
        for h, way in both:
            near_wait(h, way, True)
        for h, way in both:
            send(far(h, 3, way, False))
        for j in (1, 2):
            for h, way in both:
                far_wait(h, j, way, False)
                send(far(h, j, way, True))

    def out_round_3():
        for h, way in both:
            far_wait(h, 3, way, False)
            send(far(h, 3, way, True))

    def out_round_4():
        for j in range(4):
            for h, way in both:
                far_wait(h, j, way, True)

    def other_half():
        swap_wait(0)

    def feat_place(step, t, sub):
        return folded.at[(z - step * t + nz) % nz, (core + sub) % 2]

    def feat_far_place(step, held, t, sub):
        return feat_place(step, held, sub)

    def unfold(first, last):
        part = halves.shape[2]
        half_tokens = tokens // 2
        for t in range(first, last):
            for step in (1, -1):
                if t <= (plus if step == 1 else minus) and (t or step == 1):
                    source = (z - step * t + nz) % nz
                    sides = [folded[source, c] for c in (0, 1)]
                    for i in (0, 1):
                        feats[source, i * half_tokens : (i + 1) * half_tokens, :] = jnp.concatenate(
                            [side[:, i * part : (i + 1) * part] for side in sides], axis=1
                        )

    def whole_order(row):
        block = (row // own_tokens + (z + nz - half)) % nz
        return block * own_tokens + row % own_tokens

    def index_work():
        for copy in small_copies:
            copy.wait()
        request = lax.broadcasted_iota(jnp.int32, (slots, ndp * slots), 1)
        order = lax.broadcasted_iota(jnp.int32, (slots, ndp * slots), 0)
        spread_plan = jnp.where(request % slots == order, plan_row[...], 0).astype(bf16)
        request = lax.broadcasted_iota(jnp.int32, (ndp * slots, ndp), 0)
        holder = lax.broadcasted_iota(jnp.int32, (ndp * slots, ndp), 1)
        owner = jnp.where(request // slots == holder, 1.0, 0.0).astype(bf16)
        plan = jnp.dot(spread_plan, owner, preferred_element_type=f32)
        slot_id = lax.broadcasted_iota(jnp.int32, (slots, slots, ndp), 1) + dp * slots
        hot = jnp.broadcast_to(plan[:, None, :], (slots, slots, ndp)) == slot_id.astype(f32)
        select[...] = jnp.where(hot, 1.0, 0.0).reshape(slots * slots, ndp)
        token = lax.broadcasted_iota(jnp.int32, (tokens, ndp * slots), 0)
        lane = lax.broadcasted_iota(jnp.int32, (tokens, ndp * slots), 1)
        own_request = lane == dp * slots + whole_order(token) // seq
        owner_slot = jnp.sum(
            jnp.where(own_request, plan_row[...].astype(f32), 0.0), axis=1, keepdims=True
        )
        slot_hot[...] = jnp.where(lane.astype(f32) == owner_slot, 1.0, 0.0)

    def first_hook():
        for c in (0, 1):

            @pl.when(core == c)
            def _(c=c):
                theirs = refer if c == 0 else policy
                for i, place in enumerate(places(c)):
                    if i:
                        remote(theirs[i], place, swap_send.at[i], swap_recv.at[i], sibling).start()

        out_round_0()
        index_work()

    hooks = {0: first_hook, half: lambda: unfold(0, half + 1), plus - 2: out_round_1}
    tree_gather(feat_place, feat_far_place, gather_send, gather_recv, hooks, other_half)
    unfold(half + 1, plus + 1)

    for i in (4, 5):
        for c in (0, 1):

            @pl.when(core == c)
            def _(c=c, i=i):
                local_copy(c, i).wait()

    row_step = min(128, tokens)

    @pl.loop(0, tokens // row_step)
    def _(i):
        rows = pl.ds(pl.multiple_of(i * row_step, row_step), row_step)

        def store(k, tile):
            normed_in[rows, k * 128 : (k + 1) * 128] = tile

        normed_tiles(lambda k: feats[k, rows, :].astype(f32), nfeat, gains[0], width, store)

    swap_wait(2)
    swap_wait(3)
    pre = jnp.dot(normed_in[...], up[...], preferred_element_type=f32)
    active = jax.nn.gelu(pre).astype(bf16)

    sub_width = width // SUBS

    def rows_of(chunk):
        return pl.ds(pl.multiple_of(chunk * own_tokens, own_tokens), own_tokens)

    def sum_copy(way, t, sub):
        cols = slice(sub * sub_width, (sub + 1) * sub_width)
        return remote(
            sums_out.at[way, t - 1, :, cols],
            sums_in.at[way, t - 1, :, cols],
            sum_send.at[way, t - 1, sub],
            sum_recv.at[way, t - 1, sub],
            z_peer((1, -1)[way] * (1 if t % 2 else 2)),
        )

    def hand_on(t):
        for sub in range(SUBS):
            cols = slice(sub * sub_width, (sub + 1) * sub_width)
            if t == plus:
                partial[:, cols] = jnp.dot(active, down[:, cols], preferred_element_type=f32)
            for way, step in ways:
                hops = reach(way, sub)
                if t > hops:
                    continue
                term = partial[rows_of((z + step * t + nz) % nz), cols]
                if t % 2 == 0:
                    for behind in (t + 2, t + 1):
                        if behind <= hops:
                            sum_copy(way, behind, sub).wait_recv()
                            term = term + sums_in[way, behind - 1, :, cols].astype(f32)
                sums_out[way, t - 1, :, cols] = term.astype(sums_out.dtype)
                send(sum_copy(way, t, sub))

    hand_on(plus)
    for t in range(plus - 1, 2, -2):
        hand_on(t)
        if t == plus - 5:
            hand_on(plus - 2)
            out_round_2()
    for t in range(plus - 4, 0, -2):
        hand_on(t)
        if t == plus - 4:
            hand_on(1)

    for t in (1, 2):
        for sub in range(SUBS):
            for way in (0, 1):
                sum_copy(way, t, sub).wait_recv()

    mine = rows_of(z)
    for k in range(nfeat):
        cols = slice(k * 128, (k + 1) * 128)
        came = [sums_in[way, t, :, cols].astype(f32) for way in (0, 1) for t in (0, 1)]
        total = partial[mine, cols] + add_up(came)
        after[k] = feats[k, mine, :].astype(f32) + total

    def store_out(k, tile):
        normed_out[half * own_tokens : (half + 1) * own_tokens, k * 128 : (k + 1) * 128] = tile

    normed_tiles(lambda k: after[k], nfeat, gains[1], width, store_out)

    def out_place(step, t, sub):
        slot = (half - step * t + nz) % nz
        cols = slice(sub * sub_width, (sub + 1) * sub_width)
        return normed_out.at[slot * own_tokens : (slot + 1) * own_tokens, cols]

    def out_far_place(step, held, t, sub):
        return out_place(step, t, sub)

    def target_copy(i, source):
        return remote(
            wanted.at[source],
            wanted.at[source],
            target_send,
            target_recv,
            ((dp + i) % ndp, mp),
        )

    def send_targets():
        out_round_4()
        for i in range(1, ndp):
            target_copy(i, dp).start()

    def settle_early():
        for i in range(4):
            swap_done(i)
        settle(early)

    def target_work():
        others = wanted.at[0 : ndp - 1]
        every = remote(others, others, target_send, target_recv, sibling)
        every.wait_send()
        every.wait_recv()
        all_targets = wanted[...].astype(f32).reshape(ndp * slots, seq)
        seen = jnp.dot(slot_hot[...], all_targets, precision=HIGH, preferred_element_type=f32)
        position = lax.broadcasted_iota(jnp.int32, (tokens, seq), 1)
        row = lax.broadcasted_iota(jnp.int32, (tokens, seq), 0)
        target_col[...] = jnp.sum(
            jnp.where(position == whole_order(row) % seq, seen, 0.0), axis=1, keepdims=True
        ).astype(jnp.int32)

    block = 256
    ntile = 2 * vocab // 128

    def score(first, last):
        rows = slice(first * own_tokens, last * own_tokens)

        @pl.loop(0, 2 * vocab // block)
        def _(i):
            cols = pl.ds(pl.multiple_of(i * block, block), block)
            logits[rows, cols] = jnp.dot(
                normed_out[rows, :], out[:, cols], preferred_element_type=f32
            )

    def summarize(first, last):
        rows = slice(first * own_tokens, last * own_tokens)
        shape = ((last - first) * own_tokens, 128)

        def load(k):
            return logits[rows, k * 128 : (k + 1) * 128]

        top = load(0)
        for k in range(1, ntile):
            top = jnp.maximum(top, load(k))
        top = jnp.max(top, axis=1, keepdims=True)
        place = lax.broadcasted_iota(jnp.int32, shape, 1)
        spot = target_col[rows, :] - z * (2 * vocab) - place
        total = jnp.zeros(shape, f32)
        hits = jnp.zeros(shape, f32)
        for k in range(ntile):
            tile = load(k)
            total = total + jnp.exp(tile - top)
            hits = hits + jnp.where(spot == k * 128, tile, 0.0)
        local = top + jnp.log(jnp.sum(total, axis=1, keepdims=True))
        picked = jnp.sum(hits, axis=1, keepdims=True)
        values = jnp.where(place == 0, local, jnp.where(place == 1, picked, 0.0))
        for i in range(first, last):
            block_rows = values[(i - first) * own_tokens : (i - first + 1) * own_tokens]
            columns[rows_of((z + i + nz - half) % nz), :] = block_rows

    def summarize_all(first, last):
        for i in range(first, last, 3):
            summarize(i, min(i + 3, last))

    near_blocks = 2 * half + 1

    def before_far():
        target_work()
        summarize_all(0, near_blocks)

    def after_relay():
        send_targets()
        settle_early()

    early = list(waits)
    waits.clear()
    hooks = {
        0: out_round_3,
        2: after_relay,
        half: lambda: score(0, near_blocks),
        plus - 2: before_far,
    }
    tree_gather(out_place, out_far_place, spread_send, spread_recv, hooks)
    score(near_blocks, nz)
    summarize_all(near_blocks, nz)

    turned = columns[...].T
    ngroup = tokens // 128
    for g in range(ngroup):
        stats[z, g : g + 1, :] = turned[0:1, g * 128 : (g + 1) * 128]
        stats[z, ngroup + g : ngroup + g + 1, :] = turned[1:2, g * 128 : (g + 1) * 128]

    for i in far_first_z:
        remote(stats.at[z], stats.at[z], stat_send, stat_recv, z_peer(i)).start()
    settle(waits)
    others = stats.at[0 : nz - 1]
    every = remote(others, others, stat_send, stat_recv, z_peer(1))
    every.wait_send()
    every.wait_recv()
    parts = [stats[i] for i in range(nz)]
    sums = [part[:ngroup] for part in parts]
    top = sums[0]
    for part in sums[1:]:
        top = jnp.maximum(top, part)
    total = add_up([jnp.exp(part - top) for part in sums])
    picked = add_up([part[ngroup:] for part in parts])
    lps[core * ndp + dp] = picked - (top + jnp.log(total))

    place = lps.at[core * ndp + dp]
    for step in far_first_dp + [0]:
        for turn in (0, 1):
            if step or turn:
                peer = ((x + step // SIDE) % SIDE) * SIDE + (y + step % SIDE) % SIDE
                device = (peer, z * 2 + (core + turn) % 2)
                remote(place, place, lp_send, lp_recv, device).start()
    others = lps.at[0 : 2 * ndp - 1]
    every = remote(others, others, lp_send, lp_recv, sibling)
    every.wait_recv()

    per_group = slots // ngroup
    taken = []
    for g in range(ngroup):
        hot = select[g * per_group * slots : (g + 1) * per_group * slots, :]
        between = lps[:ndp, g, :] - lps[ndp:, g, :]
        got = jnp.dot(hot, between, precision=HIGH, preferred_element_type=f32)
        row = lax.broadcasted_iota(jnp.int32, got.shape, 0) // slots
        lane = lax.broadcasted_iota(jnp.int32, got.shape, 1) // seq
        got = jnp.where(row == lane, got, 0.0)
        taken += [got[j * slots : (j + 1) * slots] for j in range(per_group)]
    fold = jnp.where(
        lax.broadcasted_iota(jnp.int32, (128, seq), 0) % seq
        == lax.broadcasted_iota(jnp.int32, (128, seq), 1),
        1.0,
        0.0,
    )
    moved = jnp.dot(add_up(taken), fold, precision=HIGH, preferred_element_type=f32)
    here = lax.broadcasted_iota(jnp.int32, (slots, slots), 0)
    there = lax.broadcasted_iota(jnp.int32, (slots, slots), 1)
    long = jnp.sum(jnp.where(here == there, lengths[...].astype(f32), 0.0), axis=1, keepdims=True)
    live = lax.broadcasted_iota(jnp.int32, (slots, seq), 1).astype(f32) < long
    kept = jnp.where(live, moved, 0.0)
    token_diff[...] = kept
    in_all = jnp.sum(kept, axis=1, keepdims=True)
    seq_diff[...] = jnp.sum(jnp.where(here == there, in_all, 0.0), axis=0, keepdims=True)

    every.wait_send()


def local(
    nz,
    hidden_policy,
    hidden_reference,
    ffn_gain_policy,
    ffn_gain_reference,
    up_policy,
    up_reference,
    down_policy,
    down_reference,
    final_gain_policy,
    final_gain_reference,
    out_policy,
    out_reference,
    move_plan,
    lengths,
    targets,
):
    slots, seq, part = hidden_policy.shape
    tokens = slots * seq
    width = up_policy.shape[0]
    units = up_policy.shape[1]
    vocab = out_policy.shape[1]
    ndp = SIDE * SIDE
    own = tokens // nz
    ngroup = tokens // 128
    plus = nz // 2
    any_space = pl.BlockSpec(memory_space=pl.ANY)
    vmem = pl.BlockSpec(memory_space=pltpu.VMEM)
    dma = pltpu.SemaphoreType.DMA
    ring = (2, plus, SUBS)
    token_diff, seq_diff = pl.pallas_call(
        functools.partial(kernel, nz),
        out_shape=(
            jax.ShapeDtypeStruct((slots, seq), f32),
            jax.ShapeDtypeStruct((1, slots), f32),
        ),
        in_specs=[any_space] * 15,
        out_specs=(vmem, vmem),
        scratch_shapes=[
            pltpu.VMEM((1, ndp * slots), jnp.int32),
            pltpu.VMEM((1, slots), jnp.int32),
            pltpu.VMEM((2, 1, width), f32),
            pltpu.VMEM((width // 128, own, 128), f32),
            pltpu.VMEM((2, tokens, part), bf16),
            pltpu.VMEM((tokens // 2, 2 * part), bf16),
            pltpu.VMEM((nz, 2, tokens // 2, 128), bf16),
            pltpu.VMEM((width // 128, tokens, 128), bf16),
            pltpu.VMEM((tokens, width), bf16),
            pltpu.VMEM((width, 2 * units), bf16),
            pltpu.VMEM((2 * units, width), bf16),
            pltpu.VMEM((width, 2 * vocab), bf16),
            pltpu.VMEM((tokens, width), f32),
            pltpu.VMEM((2, plus, own, width), SUM_TYPE),
            pltpu.VMEM((2, plus, own, width), SUM_TYPE),
            pltpu.VMEM((tokens, width), bf16),
            pltpu.VMEM((tokens, 2 * vocab), f32),
            pltpu.VMEM((tokens, 128), f32),
            pltpu.VMEM((ndp, slots, seq), jnp.int32),
            pltpu.VMEM((tokens, 1), jnp.int32),
            pltpu.VMEM((tokens, ndp * slots), f32),
            pltpu.VMEM((slots * slots, ndp), f32),
            pltpu.VMEM((nz, 2 * ngroup, 128), f32),
            pltpu.VMEM((2 * ndp, ngroup, 128), f32),
            dma((10,)),
            dma((4,)),
            dma((4,)),
            dma(ring),
            dma(ring),
            dma(ring),
            dma(ring),
            dma(ring),
            dma(ring),
            dma((2, 2, 2)),
            dma((2, 2, 2)),
            dma((2, 4, 2, 2)),
            dma((2, 4, 2, 2)),
            dma,
            dma,
            dma,
            dma,
            dma,
            dma,
        ],
        compiler_params=pltpu.CompilerParams(
            collective_id=0, has_side_effects=True, vmem_limit_bytes=60 * 1024 * 1024
        ),
        name="score",
    )(
        hidden_policy.reshape(tokens, part),
        hidden_reference.reshape(tokens, part),
        ffn_gain_policy.reshape(1, width),
        ffn_gain_reference.reshape(1, width),
        up_policy,
        up_reference,
        down_policy,
        down_reference,
        final_gain_policy.reshape(1, width),
        final_gain_reference.reshape(1, width),
        out_policy,
        out_reference,
        move_plan.reshape(1, ndp * slots),
        lengths.reshape(1, slots),
        targets,
    )
    def hand_over(token_in, seq_in, token_out, seq_out):
        token_out[...] = token_in[...]
        seq_out[...] = seq_in[...]

    token_diff, seq_diff = pl.pallas_call(
        hand_over,
        out_shape=(
            jax.ShapeDtypeStruct((slots, seq), f32),
            jax.ShapeDtypeStruct((1, slots), f32),
        ),
        name="hand_over",
    )(token_diff, seq_diff)
    return token_diff, seq_diff.reshape(slots)


def solution(mesh):
    nz = mesh.shape["mp"] // 2
    return jax.shard_map(
        functools.partial(local, nz),
        mesh=mesh,
        in_specs=(
            P("dp", None, "mp"),
            P("dp", None, "mp"),
            P(),
            P(),
            P(None, "mp"),
            P(None, "mp"),
            P("mp", None),
            P("mp", None),
            P(),
            P(),
            P("dp", "mp"),
            P("dp", "mp"),
            P(),
            P("dp"),
            P("dp", None),
        ),
        out_specs=(P("dp", None), P("dp")),
        check_vma=False,
    )
```
